256 devices in a mesh: tile: 8 (over z_hi, core), view: 32 (over z_lo, y, x).
Axes of the slice: x: 4, y: 4, z: 8 (z_hi: 4, z_lo: 2; z = z_hi * 2 + z_lo), core: 2. Of those that a mesh axis runs over, the one named last changes fastest.
Arguments:
- estimate: float32 [192, 1536, 128], P('tile', 'view'), may hold values from 0.5 to 1.5
- views: float32 [6, 192, 1536, 128], P(None, 'tile', 'view'), may hold values from 0.1 to 3
- background: float32 [6], replicated, may hold values from 0.1 to 1
- psf_taps: float32 [6, 3, 11], replicated, may hold values from 0.2 to 1
- psf_lengths: int32 [6, 3], replicated, may hold values from 3 to 11, as said below
- view_offsets: int32 [6, 3], replicated, may hold values from -4 to 4, as said below
- field_rows: int32 [6, 2], replicated, may hold values from 0 to 1536, as said below
Outputs:
- restored: float32 [192, 1536, 128], P('tile', 'view')
The draws below stay inside these ranges and needn't reach their ends.
Inputs may be any that keep to these rules, and one draw needn't show every extreme that they name: `psf_lengths`: odd; for each dimension some view has length 11. `view_offsets`: for each dimension some view has offset 4 and another -4. `field_rows`: the first column is at most 384 and the second at least 1152; some view starts at row 0 and some ends at row 1536.
All inputs are finite; a program needn't handle non-finite values.
Results may differ from the reference program's by a relative error of at most 0.0003.
Values sent between devices are 32-bit elements; how exact they have to be, the bound alone decides.
A program may use at most 64 MiB of HBM per device.

```python
import math
import jax
import jax.numpy as jnp
from jax import lax

VIEWS = 6
KMAX = 11
OFF = 4
LANES = 128
ITERS = 2
HALO = 9
NZ = 192
NY = 1536


def draw_psf_lengths(key, part):
    first_key, second_key = jax.random.split(jax.random.fold_in(key, 11))
    halves = jax.random.randint(first_key, (VIEWS, 3), 1, KMAX // 2 + 1)
    chosen = jax.random.randint(second_key, (3,), 0, VIEWS)
    halves = halves.at[chosen, jnp.arange(3)].set(KMAX // 2)
    return (2 * halves + 1).astype(jnp.int32)


def draw_view_offsets(key, part):
    first_key, second_key = jax.random.split(jax.random.fold_in(key, 23))
    shifts = jax.random.randint(first_key, (VIEWS, 3), -OFF, OFF + 1)
    order = jax.vmap(lambda item: jax.random.permutation(item, VIEWS))(jax.random.split(second_key, 3))
    shifts = shifts.at[order[:, 0], jnp.arange(3)].set(OFF)
    shifts = shifts.at[order[:, 1], jnp.arange(3)].set(-OFF)
    return shifts.astype(jnp.int32)


def draw_field_rows(key, part):
    first_key, second_key, third_key = jax.random.split(jax.random.fold_in(key, 37), 3)
    quarter = NY // 4
    lower = jax.random.randint(first_key, (VIEWS,), 0, quarter + 1)
    upper = NY - jax.random.randint(second_key, (VIEWS,), 0, quarter + 1)
    order = jax.random.permutation(third_key, VIEWS)
    lower = lower.at[order[0]].set(0)
    upper = upper.at[order[1]].set(NY)
    return jnp.stack([lower, upper], axis=1).astype(jnp.int32)


def levels(key, dims, shards, low, high):
    level, own = 1.0, jax.random.fold_in(key, 6)
    for axis_at, shards_of in shards:
        draws = jnp.exp(jax.random.uniform(jax.random.fold_in(own, axis_at), (shards_of,), jnp.float32, low / len(shards), high / len(shards)))
        level = level * jnp.repeat(draws, dims[axis_at] // shards_of).reshape([-1 if axis == axis_at else 1 for axis in range(len(dims))])
    return level


def setup_inputs(seed: int = 0) -> dict:
    splits = jax.random.split(jax.random.key(seed), 8)
    estimate = jnp.clip(0.5 + 1.0 * jax.random.uniform(splits[0], (NZ, NY, LANES), jnp.float32) ** levels(splits[0], (NZ, NY, LANES), ((0, 8), (1, 32)), -0.2, 0.2), 0.5, 1.5)
    views = jnp.clip(jnp.exp(math.log(3.0) - 3.4011974 * jax.random.uniform(splits[1], (VIEWS, NZ, NY, LANES), jnp.float32) ** levels(splits[1], (VIEWS, NZ, NY, LANES), ((1, 8), (2, 32)), -0.2, 0.2)), 0.1, 3.0)
    background = jnp.clip(jnp.exp(jax.random.uniform(splits[2], (VIEWS,), jnp.float32, math.log(0.1), math.log(1.0))), 0.1, 1.0)
    psf_taps = jnp.clip(jax.random.uniform(splits[3], (VIEWS, 3, KMAX), jnp.float32, 0.2, 1.0), 0.2, 1.0)
    psf_lengths = draw_psf_lengths(jax.random.fold_in(splits[7], 71), 0)
    view_offsets = draw_view_offsets(jax.random.fold_in(splits[7], 71), 0)
    field_rows = draw_field_rows(jax.random.fold_in(splits[7], 71), 0)
    return dict(estimate=estimate, views=views, background=background, psf_taps=psf_taps, psf_lengths=psf_lengths, view_offsets=view_offsets, field_rows=field_rows)


def taps_table(psf_taps, psf_lengths):
    places = jnp.arange(KMAX, dtype=jnp.int32)
    live = (places[None, None, :] < psf_lengths[:, :, None]).astype(psf_taps.dtype)
    raw = psf_taps * live
    return raw / jnp.sum(raw, axis=2, keepdims=True)


def slide(field, weights, start, axis, sign):
    size = field.shape[axis]
    widths = [(0, 0), (0, 0), (0, 0)]
    widths[axis] = (HALO, HALO)
    padded = jnp.pad(field, widths)
    total = jnp.zeros_like(field)
    for place in range(KMAX):
        begin = (HALO + sign * (start + place)).astype(jnp.int32)
        total = total + weights[place] * lax.dynamic_slice_in_dim(padded, begin, size, axis)
    return total


def reference(estimate, views, background, psf_taps, psf_lengths, view_offsets, field_rows):
    weights = taps_table(psf_taps, psf_lengths)
    start = (view_offsets - psf_lengths // 2).astype(jnp.int32)
    places = jnp.arange(estimate.shape[1], dtype=jnp.int32)
    restored = estimate
    for step in range(ITERS):
        def one_view(total, item):
            observed, level, kernel, begin, bounds = item
            blurred = restored
            for axis in range(3):
                blurred = slide(blurred, kernel[axis], begin[axis], axis, 1)
            covered = (places >= bounds[0]) & (places < bounds[1])
            ratio = jnp.where(covered[None, :, None], observed / (blurred + level), 1.0)
            spread = ratio
            for axis in range(3):
                spread = slide(spread, kernel[axis], begin[axis], axis, -1)
            return total + spread, None

        total, unused = lax.scan(one_view, jnp.zeros_like(restored), (views, background, weights, start, field_rows))
        restored = restored * total / VIEWS
    return restored
```

```python
import functools

import jax
import jax.numpy as jnp
from jax import lax
from jax.experimental import pallas as pl
from jax.experimental.pallas import tpu as pltpu
from jax.sharding import PartitionSpec as P

ITERS = 2
HALO = 9
TAPS = 11
MID = 5
PAD = 8
FAR = 10000
f32 = jnp.float32
bf16 = jnp.bfloat16


def split(x):
    high = x.astype(bf16)
    low = (x - high.astype(f32)).astype(bf16)
    return high, low


def iota(shape, dim):
    return lax.broadcasted_iota(jnp.int32, shape, dim)


def kernel(
    tiles, strips_count,
    est_hbm, views_hbm, level, taps, lengths, offsets, field,
    out_ref,
    est, obs, total, mid, wz, yf, ya, xf, xa, zb, gx, sh, sl,
    z_send, y_send, c_send, z_recv, y_recv, c_recv,
    load_sem, send_sem, recv_sem,
):
    count, depth, rows, lanes = obs.shape
    reach = depth + 2 * HALO
    top = depth - HALO
    side = HALO * depth
    t = lax.axis_index("tile")
    u = lax.axis_index("view")

    load_est = pltpu.make_async_copy(est_hbm, est, load_sem.at[0])
    load_est.start()
    load_obs = pltpu.make_async_copy(views_hbm, obs, load_sem.at[1])
    load_obs.start()

    def exists(dt, du):
        terms = []
        if dt < 0:
            terms.append(t > 0)
        if dt > 0:
            terms.append(t < tiles - 1)
        if du < 0:
            terms.append(u > 0)
        if du > 0:
            terms.append(u < strips_count - 1)
        return functools.reduce(jnp.logical_and, terms)

    around = [(dt, du) for dt in (-1, 0, 1) for du in (-1, 0, 1) if (dt, du) != (0, 0)]

    def place(dt, du):
        return (dt + 1) * 3 + du + 1

    barrier = pltpu.get_barrier_semaphore()
    expected = jnp.int32(0)
    for dt, du in around:
        there = exists(dt, du)
        expected = expected + there.astype(jnp.int32)

        @pl.when(there)
        def _():
            pl.semaphore_signal(
                barrier, inc=1, device_id=(t + dt, u + du), device_id_type=pl.DeviceIdType.MESH
            )

    for phase in range(2 * ITERS):
        for s in range(2):
            y_recv[phase, s, 0:PAD] = jnp.zeros((PAD, lanes), f32)
            y_recv[phase, s, PAD + side : 2 * PAD + side] = jnp.zeros((PAD, lanes), f32)
            y_send[phase, s, 0:PAD] = jnp.zeros((PAD, lanes), f32)

            @pl.when(jnp.logical_not(exists(2 * s - 1, 0)))
            def _():
                z_recv[phase, s] = jnp.zeros((HALO, rows, lanes), f32)

            @pl.when(jnp.logical_not(exists(0, 2 * s - 1)))
            def _():
                y_recv[phase, s, PAD : PAD + side] = jnp.zeros((side, lanes), f32)

            for r in range(2):
                k = 2 * s + r
                c_recv[phase, k, 0:PAD] = jnp.zeros((PAD, lanes), f32)
                c_recv[phase, k, 96:104] = jnp.zeros((8, lanes), f32)
                c_send[phase, k, 80:104] = jnp.zeros((24, lanes), f32)

                @pl.when(jnp.logical_not(exists(2 * s - 1, 2 * r - 1)))
                def _():
                    c_recv[phase, k, 8:96] = jnp.zeros((88, lanes), f32)

    def message(phase, dt, du):
        adjoint = phase % 2
        if du == 0:
            s = (dt + 1) // 2
            if adjoint:
                src = z_send.at[phase // 2, s]
            else:
                src = est.at[pl.ds(top * s, HALO)]
            dst = z_recv.at[phase, 1 - s]
        elif dt == 0:
            s = (du + 1) // 2
            src = y_send.at[phase, s, pl.ds(PAD, side)]
            dst = y_recv.at[phase, 1 - s, pl.ds(PAD, side)]
        else:
            s, r = (dt + 1) // 2, (du + 1) // 2
            if adjoint:
                src = c_send.at[phase, 2 * s + r, pl.ds(8, 88)]
            else:
                src = y_send.at[phase, r, pl.ds(PAD + s * (side - 88), 88)]
            dst = c_recv.at[phase, 2 * (1 - s) + 1 - r, pl.ds(8, 88)]
        return pltpu.make_async_remote_copy(
            src_ref=src,
            dst_ref=dst,
            send_sem=send_sem.at[phase, place(dt, du)],
            recv_sem=recv_sem.at[phase, place(dt, du)],
            device_id=(t + dt, u + du),
            device_id_type=pl.DeviceIdType.MESH,
        )

    def send(phase, which):
        for dt, du in which:
            @pl.when(exists(dt, du))
            def _():
                message(phase, dt, du).start()

    def receive(phase, which):
        for dt, du in which:
            @pl.when(exists(-dt, -du))
            def _():
                message(phase, dt, du).wait_recv()

    def sent(phase, which):
        for dt, du in which:
            @pl.when(exists(dt, du))
            def _():
                message(phase, dt, du).wait_send()

    along_z = [(-1, 0), (1, 0)]
    along_y = [(0, -1), (0, 1)]
    corners = [(-1, -1), (-1, 1), (1, -1), (1, 1)]

    def pack(phase):
        def body(p, carry):
            y_send[phase, 0, pl.ds(PAD + HALO * p, HALO)] = est[p, 0:HALO]
            y_send[phase, 1, pl.ds(PAD + HALO * p, HALO)] = est[p, rows - HALO : rows]
            return carry

        lax.fori_loop(0, depth, body, 0)

    load_est.wait()
    pack(0)
    pl.semaphore_wait(barrier, expected)
    send(0, along_z + corners + along_y)

    def weights_of(v, d):
        length = lengths[v, d]
        half = length // 2
        raw = []
        whole = jnp.float32(0)
        for j in range(TAPS):
            inside = j < length
            whole = whole + jnp.where(inside, taps[v, d, j], 0.0)
        scale = 1.0 / jnp.full((8, lanes), whole, f32)
        for j in range(TAPS):
            at = j - MID + half
            inside = jnp.logical_and(at >= 0, at < length)
            value = taps[v, d, jnp.clip(at, 0, TAPS - 1)]
            raw.append(jnp.where(inside, value, 0.0) * scale)
        return raw

    def filled(delta, raw):
        height, width = delta.shape
        parts = []
        for h in range(0, height, 8):
            row = []
            for w in range(0, width, 128):
                piece = delta[h : h + 8, w : w + 128]
                value = jnp.zeros(piece.shape, f32)
                for j in range(TAPS):
                    value = jnp.where(piece == j, raw[j][:, : piece.shape[1]], value)
                row.append(value)
            parts.append(jnp.concatenate(row, 1) if len(row) > 1 else row[0])
        return jnp.concatenate(parts, 0)

    def extended_place(k):
        low = k - rows
        high = k - rows - 16
        value = jnp.where(k < rows, k, FAR)
        value = jnp.where(jnp.logical_and(low >= 0, low < HALO), low - HALO, value)
        return jnp.where(jnp.logical_and(high >= 0, high < HALO), high + rows, value)

    wide = rows + 32

    def tables(v, carry):
        shift = offsets[v, 0] - MID
        raw = weights_of(v, 0)
        for j in range(TAPS):
            wz[v, j] = raw[j]
        raw = weights_of(v, 1)
        shift = offsets[v, 1] - MID
        col = iota((rows, 256), 1)
        seg = col // wide
        delta = extended_place(col - seg * wide) - iota((rows, 256), 0) - shift
        delta = jnp.where(seg < 3, delta, FAR)
        high, low = split(filled(delta, raw))
        yf[pl.ds(rows * v, rows)] = jnp.where(seg < 2, high.astype(f32), low.astype(f32)).astype(bf16)
        col = iota((wide, 256), 1)
        seg = col // rows
        delta = extended_place(iota((wide, 256), 0)) - (col - seg * rows) - shift
        delta = jnp.where(seg < 3, delta, FAR)
        high, low = split(filled(delta, raw))
        ya[v] = jnp.where(seg < 2, high.astype(f32), low.astype(f32)).astype(bf16)
        raw = weights_of(v, 2)
        shift = offsets[v, 2] - MID
        delta = iota((lanes, lanes), 0) - iota((lanes, lanes), 1)
        high, low = split(filled(delta - shift, raw))
        both = jnp.concatenate([high, low], 1)
        xf[v] = jnp.concatenate([both, both], 0)
        high, low = split(filled(-delta - shift, raw))
        both = jnp.concatenate([high, low], 1)
        xa[v] = jnp.concatenate([both, both], 0)
        for half in (sh, sl):
            half[v, 0:8] = jnp.zeros((8, rows, lanes), bf16)
            half[v, depth + 18 : depth + 26] = jnp.zeros((8, rows, lanes), bf16)
        return carry

    lax.fori_loop(0, count, tables, 0)
    load_obs.wait()

    def stacked(own, low, high):
        full = jnp.concatenate([own, low, high], 0)
        a, b = split(full)
        return jnp.concatenate([a, b, a], 0)

    def rows_pass(first, second, at_first, at_second):
        rhs = jnp.concatenate([stacked(*first), stacked(*second)], 1)
        out = jnp.dot(yf[:, : 3 * wide], rhs, preferred_element_type=f32)
        mid[at_first] = out[:, :lanes]
        mid[at_second] = out[:, lanes:]

    def inner_rows(phase):
        def body(n, carry):
            def load(p):
                at = PAD + HALO * p
                return est[p], y_recv[phase, 0, pl.ds(at, 16)], y_recv[phase, 1, pl.ds(at, 16)]

            rows_pass(load(2 * n), load(2 * n + 1), HALO + 2 * n, HALO + 2 * n + 1)
            return carry

        lax.fori_loop(0, depth // 2, body, 0)

    def outer_rows(phase):
        def body(n, carry):
            def load(s):
                at = PAD + HALO * n + (7 if s == 0 else 0)
                return (
                    z_recv[phase, s, n],
                    c_recv[phase, 2 * s, pl.ds(at, 16)],
                    c_recv[phase, 2 * s + 1, pl.ds(at, 16)],
                )

            rows_pass(load(0), load(1), n, HALO + depth + n)
            return carry

        lax.fori_loop(0, HALO, body, 0)

    first_row = u * rows
    span = depth // 3

    def one_view(v, carry):
        base = offsets[v, 0] + MID - 1
        w = [wz[v, j] for j in range(TAPS)]

        def forward_depth(g, carry):
            at = pl.multiple_of(16 * g, 16)
            left = pl.multiple_of(rows * v + 16 * g, 16)
            window = []
            for i in range(depth + TAPS - 1):
                block = mid[base + i, pl.ds(left, 16)]
                window.append((block[:8], block[8:]))
                if i >= TAPS - 1:
                    p = i - TAPS + 1
                    halves = []
                    for h in range(2):
                        value = w[0] * window[p][h]
                        for j in range(1, TAPS):
                            value = value + w[j] * window[p + j][h]
                        halves.append(value)
                    a, b = split(jnp.concatenate(halves, 0))
                    zb[p, pl.ds(at, 16), :lanes] = a
                    zb[p, pl.ds(at, 16), lanes:] = b
            return carry

        lax.fori_loop(0, rows // 16, forward_depth, 0)

        place_y = first_row + iota((rows, lanes), 0)
        covered = jnp.logical_and(place_y >= field[v, 0], place_y < field[v, 1])
        back = level[v]

        def along_x(c, carry):
            part = pl.ds(span * c, span)
            lhs = zb[part].reshape(span * rows, 2 * lanes)
            out = jnp.dot(lhs, xf[v], preferred_element_type=f32)
            blurred = out[:, :lanes] + out[:, lanes:]
            blurred = blurred.reshape(span, rows, lanes)
            ratio = jnp.where(covered[None], obs[v, part] / (blurred + back), 1.0)
            a, b = split(ratio.reshape(span * rows, lanes))
            out = jnp.dot(jnp.concatenate([a, b], 1), xa[v], preferred_element_type=f32)
            gx[part] = (out[:, :lanes] + out[:, lanes:]).reshape(span, rows, lanes)
            return carry

        lax.fori_loop(0, 3, along_x, 0)

        def adjoint_depth(g, carry):
            at = pl.multiple_of(16 * g, 16)
            window = {}
            for i in range(depth + TAPS - 1):
                if i < depth:
                    block = gx[i, pl.ds(at, 16)]
                    window[i] = (block[:8], block[8:])
                halves = []
                for h in range(2):
                    terms = [w[j] * window[i - j][h] for j in range(TAPS) if 0 <= i - j < depth]
                    halves.append(functools.reduce(lambda x, y: x + y, terms))
                a, b = split(jnp.concatenate(halves, 0))
                sh[v, 8 + i, pl.ds(at, 16)] = a
                sl[v, 8 + i, pl.ds(at, 16)] = b
            return carry

        lax.fori_loop(0, rows // 16, adjoint_depth, 0)
        return carry

    def rows_adjoint(first, second):
        acc = None
        for v in range(count):
            cols = []
            for p in (first, second):
                at = p + MID - 1 - offsets[v, 0]
                a, b = sh[v, at], sl[v, at]
                cols.append(jnp.concatenate([a, b, a], 0))
            out = jnp.dot(ya[v, :, : 3 * rows], jnp.concatenate(cols, 1), preferred_element_type=f32)
            acc = out if acc is None else acc + out
        return acc

    def outer_adjoint(phase):
        def body(n, carry):
            acc = rows_adjoint(n, HALO + depth + n)
            for s in range(2):
                half = acc[:, s * lanes : (s + 1) * lanes]
                z_send[phase // 2, s, n] = half[:rows]
                for r in range(2):
                    c_send[phase, 2 * s + r, pl.ds(PAD + HALO * n, 16)] = half[rows + 16 * r : rows + 16 * r + 16]
            return carry

        lax.fori_loop(0, HALO, body, 0)

    def inner_adjoint(phase):
        def body(n, carry):
            acc = rows_adjoint(HALO + 2 * n, HALO + 2 * n + 1)
            for s in range(2):
                p = 2 * n + s
                half = acc[:, s * lanes : (s + 1) * lanes]
                total[p] = half[:rows]
                for r in range(2):
                    y_send[phase, r, pl.ds(PAD + HALO * p, 16)] = half[rows + 16 * r : rows + 16 * r + 16]
            return carry

        lax.fori_loop(0, depth // 2, body, 0)

    early = iota((16, lanes), 0) < HALO
    late = iota((16, lanes), 0) >= 16 - HALO

    def update(phase, target):
        def plane(p, s, n):
            value = total[p]
            head, body, tail = value[:16], value[16 : rows - 16], value[rows - 16 :]
            head = head + jnp.where(early, y_recv[phase, 0, pl.ds(PAD + HALO * p, 16)], 0.0)
            tail = tail + jnp.where(late, y_recv[phase, 1, pl.ds(1 + HALO * p, 16)], 0.0)
            if s is not None:
                head = head + jnp.where(early, c_recv[phase, 2 * s, pl.ds(PAD + HALO * n, 16)], 0.0)
                tail = tail + jnp.where(late, c_recv[phase, 2 * s + 1, pl.ds(1 + HALO * n, 16)], 0.0)
            value = jnp.concatenate([head, body, tail], 0)
            if s is not None:
                value = value + z_recv[phase, s, n]
            target[p] = est[p] * value * (1.0 / count)

        def low(n, carry):
            plane(n, 0, n)
            return carry

        def middle(n, carry):
            plane(n, None, None)
            return carry

        def high(n, carry):
            plane(top + n, 1, n)
            return carry

        lax.fori_loop(0, HALO, low, 0)
        lax.fori_loop(HALO, top, middle, 0)
        lax.fori_loop(0, HALO, high, 0)

    for step in range(ITERS):
        ahead, back = 2 * step, 2 * step + 1
        receive(ahead, along_y)
        inner_rows(ahead)
        receive(ahead, along_z + corners)
        outer_rows(ahead)
        lax.fori_loop(0, count, one_view, 0)
        outer_adjoint(back)
        send(back, along_z + corners)
        inner_adjoint(back)
        send(back, along_y)
        receive(back, along_y + along_z + corners)
        sent(ahead, along_y + along_z + corners)
        if step < ITERS - 1:
            update(back, est)
            pack(ahead + 2)
            send(ahead + 2, along_z + corners + along_y)
        else:
            update(back, out_ref)
        sent(back, along_y + along_z + corners)


def solution(mesh):
    tiles, strips_count = mesh.shape["tile"], mesh.shape["view"]

    def on_device(estimate, views, background, psf_taps, psf_lengths, view_offsets, field_rows):
        count, depth, rows, lanes = views.shape
        reach = depth + 2 * HALO
        side = HALO * depth
        phases = 2 * ITERS
        anywhere = pl.BlockSpec(memory_space=pl.ANY)
        scalar = pl.BlockSpec(memory_space=pltpu.SMEM)
        v = pltpu.VMEM
        return pl.pallas_call(
            functools.partial(kernel, tiles, strips_count),
            out_shape=jax.ShapeDtypeStruct((depth, rows, lanes), f32),
            in_specs=[anywhere, anywhere] + [scalar] * 5,
            out_specs=pl.BlockSpec(memory_space=pltpu.VMEM),
            scratch_shapes=[
                v((depth, rows, lanes), f32),
                v((count, depth, rows, lanes), f32),
                v((depth, rows, lanes), f32),
                v((reach, count * rows, lanes), f32),
                v((count, TAPS, 8, lanes), f32),
                v((count * rows, 256), bf16),
                v((count, rows + 32, 256), bf16),
                v((count, 2 * lanes, 2 * lanes), bf16),
                v((count, 2 * lanes, 2 * lanes), bf16),
                v((depth, rows, 2 * lanes), bf16),
                v((depth, rows, lanes), f32),
                v((count, depth + 26, rows, lanes), bf16),
                v((count, depth + 26, rows, lanes), bf16),
                v((ITERS, 2, HALO, rows, lanes), f32),
                v((phases, 2, side + 2 * PAD, lanes), f32),
                v((phases, 4, 104, lanes), f32),
                v((phases, 2, HALO, rows, lanes), f32),
                v((phases, 2, side + 2 * PAD, lanes), f32),
                v((phases, 4, 104, lanes), f32),
                pltpu.SemaphoreType.DMA((2,)),
                pltpu.SemaphoreType.DMA((phases, 9)),
                pltpu.SemaphoreType.DMA((phases, 9)),
            ],
            compiler_params=pltpu.CompilerParams(
                collective_id=0, has_side_effects=True, vmem_limit_bytes=60 * 2**20
            ),
            name="deconvolve",
        )(estimate, views, background, psf_taps, psf_lengths, view_offsets, field_rows)

    return jax.shard_map(
        on_device,
        mesh=mesh,
        in_specs=(P("tile", "view", None), P(None, "tile", "view", None), P(), P(), P(), P(), P()),
        out_specs=P("tile", "view", None),
        check_vma=False,
    )
```

```python
import functools

import jax
import jax.numpy as jnp
from jax import lax
from jax.experimental import pallas as pl
from jax.experimental.pallas import tpu as pltpu
from jax.sharding import PartitionSpec as P

ITERS = 2
HALO = 9
TAPS = 11
MID = 5
PAD = 8
FAR = 10000
f32 = jnp.float32
bf16 = jnp.bfloat16


def split(x):
    high = x.astype(bf16)
    low = (x - high.astype(f32)).astype(bf16)
    return high, low


def iota(shape, dim):
    return lax.broadcasted_iota(jnp.int32, shape, dim)


def kernel(
    tiles, strips_count,
    est_hbm, views_hbm, level, taps, lengths, offsets, field,
    out_ref,
    est, obs, wide_in, mid, back_mid, wide_out, zf_build, za_build, zf, za, yf, ya, xf, xa,
    zb, rb, gh, gl,
    z_send, y_send, c_send, z_recv, y_recv, c_recv,
    load_sem, send_sem, recv_sem,
):
    count, depth, rows, lanes = obs.shape
    reach = depth + 2 * HALO
    top = depth - HALO
    pitch = rows + 2 * HALO + 1
    planes = -(-reach // 16) * 16
    side = HALO * depth
    t = lax.axis_index("tile")
    u = lax.axis_index("view")

    load_est = pltpu.make_async_copy(est_hbm, est, load_sem.at[0])
    load_est.start()
    load_obs = pltpu.make_async_copy(views_hbm, obs, load_sem.at[1])
    load_obs.start()

    def exists(dt, du):
        terms = []
        if dt < 0:
            terms.append(t > 0)
        if dt > 0:
            terms.append(t < tiles - 1)
        if du < 0:
            terms.append(u > 0)
        if du > 0:
            terms.append(u < strips_count - 1)
        return functools.reduce(jnp.logical_and, terms)

    around = [(dt, du) for dt in (-1, 0, 1) for du in (-1, 0, 1) if (dt, du) != (0, 0)]

    def place(dt, du):
        return (dt + 1) * 3 + du + 1

    barrier = pltpu.get_barrier_semaphore()
    expected = jnp.int32(0)
    for dt, du in around:
        there = exists(dt, du)
        expected = expected + there.astype(jnp.int32)

        @pl.when(there)
        def _():
            pl.semaphore_signal(
                barrier, inc=1, device_id=(t + dt, u + du), device_id_type=pl.DeviceIdType.MESH
            )

    def message(phase, dt, du):
        adjoint = phase % 2
        if du == 0:
            s = (dt + 1) // 2
            if adjoint:
                src = z_send.at[phase // 2, s]
            else:
                src = est.at[pl.ds(top * s, HALO)]
            dst = z_recv.at[phase, 1 - s]
        elif dt == 0:
            s = (du + 1) // 2
            src = y_send.at[phase, s, pl.ds(PAD, side)]
            dst = y_recv.at[phase, 1 - s, pl.ds(PAD, side)]
        else:
            s, r = (dt + 1) // 2, (du + 1) // 2
            if adjoint:
                src = c_send.at[phase, 2 * s + r, pl.ds(8, 88)]
            else:
                src = y_send.at[phase, r, pl.ds(PAD + s * (side - 88), 88)]
            dst = c_recv.at[phase, 2 * (1 - s) + 1 - r, pl.ds(8, 88)]
        return pltpu.make_async_remote_copy(
            src_ref=src,
            dst_ref=dst,
            send_sem=send_sem.at[phase, place(dt, du)],
            recv_sem=recv_sem.at[phase, place(dt, du)],
            device_id=(t + dt, u + du),
            device_id_type=pl.DeviceIdType.MESH,
        )

    def send(phase, which):
        for dt, du in which:
            @pl.when(exists(dt, du))
            def _():
                message(phase, dt, du).start()

    def receive(phase, which):
        for dt, du in which:
            @pl.when(exists(-dt, -du))
            def _():
                message(phase, dt, du).wait_recv()

    def sent(phase, which):
        for dt, du in which:
            @pl.when(exists(dt, du))
            def _():
                message(phase, dt, du).wait_send()

    along_z = [(-1, 0), (1, 0)]
    along_y = [(0, -1), (0, 1)]
    corners = [(-1, -1), (-1, 1), (1, -1), (1, 1)]

    def pack(phase):
        def body(p, carry):
            y_send[phase, 0, pl.ds(PAD + HALO * p, HALO)] = est[p, 0:HALO]
            y_send[phase, 1, pl.ds(PAD + HALO * p, HALO)] = est[p, rows - HALO : rows]
            return carry

        lax.fori_loop(0, depth, body, 0)

    load_est.wait()
    pack(0)
    pl.semaphore_wait(barrier, expected)
    send(0, along_z + corners + along_y)

    for phase in range(2 * ITERS):
        for s in range(2):
            y_recv[phase, s, 0:PAD] = jnp.zeros((PAD, lanes), f32)
            y_recv[phase, s, PAD + side : 2 * PAD + side] = jnp.zeros((PAD, lanes), f32)
            y_send[phase, s, 0:PAD] = jnp.zeros((PAD, lanes), f32)

            @pl.when(jnp.logical_not(exists(2 * s - 1, 0)))
            def _():
                z_recv[phase, s] = jnp.zeros((HALO, rows, lanes), f32)

            @pl.when(jnp.logical_not(exists(0, 2 * s - 1)))
            def _():
                y_recv[phase, s, PAD : PAD + side] = jnp.zeros((side, lanes), f32)

            for r in range(2):
                k = 2 * s + r
                c_recv[phase, k, 0:PAD] = jnp.zeros((PAD, lanes), f32)
                c_recv[phase, k, 96:104] = jnp.zeros((8, lanes), f32)
                c_send[phase, k, 80:104] = jnp.zeros((24, lanes), f32)

                @pl.when(jnp.logical_not(exists(2 * s - 1, 2 * r - 1)))
                def _():
                    c_recv[phase, k, 8:96] = jnp.zeros((88, lanes), f32)

    def weights_of(v, d):
        length = lengths[d, v]
        half = length // 2
        raw = []
        whole = jnp.float32(0)
        for j in range(TAPS):
            inside = j < length
            whole = whole + jnp.where(inside, taps[v, d, j], 0.0)
        scale = 1.0 / jnp.full((8, lanes), whole, f32)
        for j in range(TAPS):
            at = j - MID + half
            inside = jnp.logical_and(at >= 0, at < length)
            value = taps[v, d, jnp.clip(at, 0, TAPS - 1)]
            raw.append(jnp.where(inside, value, 0.0) * scale)
        return raw

    def filled(delta, raw):
        height, width = delta.shape
        parts = []
        for h in range(0, height, 8):
            row = []
            for w in range(0, width, 128):
                piece = delta[h : h + 8, w : w + 128]
                value = jnp.zeros(piece.shape, f32)
                for j in range(TAPS):
                    value = jnp.where(piece == j, raw[j], value)
                row.append(value)
            parts.append(jnp.concatenate(row, 1) if len(row) > 1 else row[0])
        return jnp.concatenate(parts, 0)

    def segmented(delta, seg, raw):
        high, low = split(filled(jnp.where(seg < 3, delta, FAR), raw))
        return jnp.where(seg < 2, high.astype(f32), low.astype(f32))

    sums = count * depth
    tall = -(-(rows + 2 * HALO) // 16) * 16
    za_build[...] = jnp.zeros(za_build.shape, f32)

    def tables(v, carry):
        shift = offsets[0, v] + MID - 1
        raw = weights_of(v, 0)
        shape = (depth, zf_build.shape[1])
        col = iota(shape, 1)
        seg = col // planes
        zf_build[pl.ds(pl.multiple_of(depth * v, 8), depth)] = segmented(
            col - seg * planes - iota(shape, 0) - shift, seg, raw
        )
        shape = za_build.shape
        col = iota(shape, 1)
        seg = col // sums
        own = col - seg * sums
        view = own // depth
        delta = iota(shape, 0) - (own - view * depth) - shift
        za_build[...] += segmented(jnp.where(view == v, delta, FAR), seg, raw)
        raw = weights_of(v, 1)
        shift = offsets[1, v] + MID - 1
        shape = (rows, yf.shape[2])
        col = iota(shape, 1)
        seg = col // tall
        yf[v] = segmented(col - seg * tall - iota(shape, 0) - shift, seg, raw).astype(bf16)
        shape = (tall, ya.shape[2])
        col = iota(shape, 1)
        seg = col // rows
        ya[v] = segmented(iota(shape, 0) - (col - seg * rows) - shift, seg, raw).astype(bf16)
        raw = weights_of(v, 2)
        shift = offsets[2, v] - MID
        delta = iota((lanes, lanes), 0) - iota((lanes, lanes), 1)
        high, low = split(filled(delta - shift, raw))
        both = jnp.concatenate([high, low], 1)
        xf[v] = jnp.concatenate([both, both], 0)
        high, low = split(filled(-delta - shift, raw))
        both = jnp.concatenate([high, low], 1)
        xa[v] = jnp.concatenate([both, both], 0)
        return carry

    lax.fori_loop(0, count, tables, 0)
    zf[...] = zf_build[...].astype(bf16)
    za[...] = za_build[...].astype(bf16)

    def clear(n, carry):
        mid[pl.ds(pl.multiple_of(64 * n, 64), 64)] = jnp.zeros((64, lanes), f32)
        return carry

    lax.fori_loop(0, mid.shape[0] // 64, clear, 0)
    extra = wide_in.shape[0] - reach * pitch
    wide_in[reach * pitch :] = jnp.zeros((extra, lanes), f32)
    load_obs.wait()

    def tripled(x):
        a, b = split(x)
        return jnp.concatenate([a, b, a], 0)

    def gather_own():
        def body(p, carry):
            wide_in[pl.ds(pitch * (HALO + p) + HALO, rows)] = est[p]
            return carry

        lax.fori_loop(0, depth, body, 0)

    def gather_y(phase):
        def body(p, carry):
            for r in range(2):
                strip = y_recv[phase, r, pl.ds(PAD + HALO * p, HALO)]
                wide_in[pl.ds(pitch * (HALO + p) + (HALO + rows) * r, HALO)] = strip
            return carry

        lax.fori_loop(0, depth, body, 0)

    def gather_z(phase):
        def body(n, carry):
            for s in range(2):
                at = pitch * (n + (HALO + depth) * s)
                wide_in[pl.ds(at + HALO, rows)] = z_recv[phase, s, n]
                for r in range(2):
                    start = PAD + HALO * n + (7 if s == 0 else 0)
                    strip = c_recv[phase, 2 * s + r, pl.ds(start, HALO)]
                    wide_in[pl.ds(at + (HALO + rows) * r, HALO)] = strip
            return carry

        lax.fori_loop(0, HALO, body, 0)

    def forward_z(n, carry):
        for k in range(11):
            y = 22 * n + 2 * k
            pair = [tripled(wide_in[pl.ds(y + i, planes, stride=pitch)]) for i in range(2)]
            out = jnp.dot(zf[:, : 3 * planes], jnp.concatenate(pair, 1), preferred_element_type=f32)
            for i in range(2):
                mid[pl.ds(y + i, sums, stride=pitch)] = out[:, i * lanes : (i + 1) * lanes]
        return carry

    first_row = u * rows
    group = 8
    groups = depth // group

    steps = count * groups

    def spread_rows(n):
        v = n // groups
        at = depth * v + group * (n - v * groups)
        table = ya[v, :, : 3 * rows]
        for k in range(group // 2):
            pair = []
            for i in range(2):
                part = pl.ds((2 * k + i) * rows, rows)
                a, b = gh[part], gl[part]
                pair.append(jnp.concatenate([a, b, a], 0))
            out = jnp.dot(table, jnp.concatenate(pair, 1), preferred_element_type=f32)
            for i in range(2):
                back_mid[pl.ds(pitch * (at + 2 * k + i), 72)] = out[:72, i * lanes : (i + 1) * lanes]

    def spread_lanes(n):
        out = jnp.dot(rb[...], xa[n // groups], preferred_element_type=f32)
        gh[...], gl[...] = split(out[:, :lanes] + out[:, lanes:])

    def compare(n):
        v = n // groups
        c = n - v * groups
        place_y = first_row + iota((rows, lanes), 0)
        covered = jnp.logical_and(place_y >= field[0, v], place_y < field[1, v])
        back = level[v]
        out = jnp.dot(zb[...], xf[v], preferred_element_type=f32)
        for k in range(group):
            part = out[k * rows : (k + 1) * rows]
            blurred = part[:, :lanes] + part[:, lanes:]
            ratio = jnp.where(covered, obs[v, group * c + k] / (blurred + back), 1.0)
            rb[k * rows : (k + 1) * rows, :lanes], rb[k * rows : (k + 1) * rows, lanes:] = split(ratio)

    def blur_rows(n):
        v = n // groups
        at = depth * v + group * (n - v * groups)
        table = yf[v, :, : 3 * tall]
        for k in range(group // 2):
            pair = [tripled(mid[pl.ds(pitch * (at + 2 * k + i), tall)]) for i in range(2)]
            out = jnp.dot(table, jnp.concatenate(pair, 1), preferred_element_type=f32)
            for i in range(2):
                part = pl.ds((2 * k + i) * rows, rows)
                zb[part, :lanes], zb[part, lanes:] = split(out[:, i * lanes : (i + 1) * lanes])

    def middle(n, carry):
        for late_by, stage in ((3, spread_rows), (2, spread_lanes), (1, compare), (0, blur_rows)):
            stage(jnp.clip(n - late_by, 0, steps - 1))
        return carry

    def adjoint_z(n, carry):
        for k in range(11):
            y = 22 * n + 2 * k
            pair = [tripled(back_mid[pl.ds(y + i, sums, stride=pitch)]) for i in range(2)]
            out = jnp.dot(za[:, : 3 * sums], jnp.concatenate(pair, 1), preferred_element_type=f32)
            for i in range(2):
                wide_out[pl.ds(y + i, planes, stride=pitch)] = out[:, i * lanes : (i + 1) * lanes]
        return carry

    def pack_outer(phase):
        def body(n, carry):
            for s in range(2):
                at = pitch * (n + (HALO + depth) * s)
                z_send[phase // 2, s, n] = wide_out[pl.ds(at + HALO, rows)]
                for r in range(2):
                    strip = wide_out[pl.ds(at + (HALO + rows) * r, HALO)]
                    c_send[phase, 2 * s + r, pl.ds(PAD + HALO * n, HALO)] = strip
            return carry

        lax.fori_loop(0, HALO, body, 0)

    def pack_inner(phase):
        def body(p, carry):
            for r in range(2):
                strip = wide_out[pl.ds(pitch * (HALO + p) + (HALO + rows) * r, HALO)]
                y_send[phase, r, pl.ds(PAD + HALO * p, HALO)] = strip
            return carry

        lax.fori_loop(0, depth, body, 0)

    early = iota((16, lanes), 0) < HALO
    late = iota((16, lanes), 0) >= 16 - HALO

    def update(phase, target):
        def plane(p, s, n):
            value = wide_out[pl.ds(pitch * (HALO + p) + HALO, rows)]
            head, body, tail = value[:16], value[16 : rows - 16], value[rows - 16 :]
            head = head + jnp.where(early, y_recv[phase, 0, pl.ds(PAD + HALO * p, 16)], 0.0)
            tail = tail + jnp.where(late, y_recv[phase, 1, pl.ds(1 + HALO * p, 16)], 0.0)
            if s is not None:
                head = head + jnp.where(early, c_recv[phase, 2 * s, pl.ds(PAD + HALO * n, 16)], 0.0)
                tail = tail + jnp.where(late, c_recv[phase, 2 * s + 1, pl.ds(1 + HALO * n, 16)], 0.0)
            value = jnp.concatenate([head, body, tail], 0)
            if s is not None:
                value = value + z_recv[phase, s, n]
            target[p] = est[p] * value * (1.0 / count)

        def low(n, carry):
            plane(n, 0, n)
            return carry

        def central(n, carry):
            plane(n, None, None)
            return carry

        def high(n, carry):
            plane(top + n, 1, n)
            return carry

        lax.fori_loop(0, HALO, low, 0)
        lax.fori_loop(HALO, top, central, 0)
        lax.fori_loop(0, HALO, high, 0)

    for step in range(ITERS):
        ahead, back = 2 * step, 2 * step + 1
        gather_own()
        receive(ahead, along_y)
        gather_y(ahead)
        receive(ahead, along_z + corners)
        gather_z(ahead)
        lax.fori_loop(0, pitch // 22, forward_z, 0)
        lax.fori_loop(0, steps + 3, middle, 0)
        lax.fori_loop(0, pitch // 22, adjoint_z, 0)
        pack_outer(back)
        send(back, along_z + corners)
        pack_inner(back)
        send(back, along_y)
        receive(back, along_y + along_z + corners)
        sent(ahead, along_y + along_z + corners)
        if step < ITERS - 1:
            update(back, est)
            pack(ahead + 2)
            send(ahead + 2, along_z + corners + along_y)
        else:
            update(back, out_ref)
        sent(back, along_y + along_z + corners)


def solution(mesh):
    tiles, strips_count = mesh.shape["tile"], mesh.shape["view"]

    def on_device(estimate, views, background, psf_taps, psf_lengths, view_offsets, field_rows):
        count, depth, rows, lanes = views.shape
        reach = depth + 2 * HALO
        side = HALO * depth
        phases = 2 * ITERS
        pitch = rows + 2 * HALO + 1
        planes = -(-reach // 16) * 16
        tall = -(-(rows + 2 * HALO) // 16) * 16
        sums = count * depth
        anywhere = pl.BlockSpec(memory_space=pl.ANY)
        scalar = pl.BlockSpec(memory_space=pltpu.SMEM)
        v = pltpu.VMEM
        return pl.pallas_call(
            functools.partial(kernel, tiles, strips_count),
            out_shape=jax.ShapeDtypeStruct((depth, rows, lanes), f32),
            in_specs=[anywhere, anywhere] + [scalar] * 5,
            out_specs=pl.BlockSpec(memory_space=pltpu.VMEM),
            scratch_shapes=[
                v((depth, rows, lanes), f32),
                v((count, depth, rows, lanes), f32),
                v((planes * pitch + 8, lanes), f32),
                v((-(-(sums * pitch + 16) // 64) * 64, lanes), f32),
                v((sums * pitch + 16, lanes), f32),
                v((planes * pitch + 8, lanes), f32),
                v((sums, 256), f32),
                v((planes, 512), f32),
                v((sums, 256), bf16),
                v((planes, 512), bf16),
                v((count, rows, 256), bf16),
                v((count, tall, 256), bf16),
                v((count, 2 * lanes, 2 * lanes), bf16),
                v((count, 2 * lanes, 2 * lanes), bf16),
                v((8 * rows, 2 * lanes), bf16),
                v((8 * rows, 2 * lanes), bf16),
                v((8 * rows, lanes), bf16),
                v((8 * rows, lanes), bf16),
                v((ITERS, 2, HALO, rows, lanes), f32),
                v((phases, 2, side + 2 * PAD, lanes), f32),
                v((phases, 4, 104, lanes), f32),
                v((phases, 2, HALO, rows, lanes), f32),
                v((phases, 2, side + 2 * PAD, lanes), f32),
                v((phases, 4, 104, lanes), f32),
                pltpu.SemaphoreType.DMA((2,)),
                pltpu.SemaphoreType.DMA((phases, 9)),
                pltpu.SemaphoreType.DMA((phases, 9)),
            ],
            compiler_params=pltpu.CompilerParams(
                collective_id=0, has_side_effects=True, vmem_limit_bytes=60 * 2**20
            ),
            name="deconvolve",
        )(estimate, views, background, psf_taps, psf_lengths.T, view_offsets.T, field_rows.T)

    return jax.shard_map(
        on_device,
        mesh=mesh,
        in_specs=(P("tile", "view", None), P(None, "tile", "view", None), P(), P(), P(), P(), P()),
        out_specs=P("tile", "view", None),
        check_vma=False,
    )
```

```python
import functools

import jax
import jax.numpy as jnp
from jax import lax
from jax.experimental import pallas as pl
from jax.experimental.pallas import tpu as pltpu
from jax.sharding import PartitionSpec as P

ITERS = 2
HALO = 9
TAPS = 11
MID = 5
PAD = 8
FAR = 10000
f32 = jnp.float32
bf16 = jnp.bfloat16


def split(x):
    high = x.astype(bf16)
    low = (x - high.astype(f32)).astype(bf16)
    return high, low


def iota(shape, dim):
    return lax.broadcasted_iota(jnp.int32, shape, dim)


def kernel(
    tiles, strips_count,
    est_hbm, views_hbm, level, taps, lengths, offsets, field,
    out_ref,
    est, obs, wide_in, mid, back_mid, wide_out, zf_build, za_build, zf, za, yf, ya, xf, xa,
    zb, rb, gh, gl,
    z_send, y_send, c_send, z_recv, y_recv, c_recv,
    load_sem, send_sem, recv_sem,
):
    count, depth, rows, lanes = obs.shape
    reach = depth + 2 * HALO
    top = depth - HALO
    pitch = rows + 2 * HALO + 1
    planes = -(-reach // 16) * 16
    side = HALO * depth
    t = lax.axis_index("tile")
    u = lax.axis_index("view")

    load_est = pltpu.make_async_copy(est_hbm, est, load_sem.at[0])
    load_est.start()
    load_obs = pltpu.make_async_copy(views_hbm, obs, load_sem.at[1])
    load_obs.start()

    def exists(dt, du):
        terms = []
        if dt < 0:
            terms.append(t > 0)
        if dt > 0:
            terms.append(t < tiles - 1)
        if du < 0:
            terms.append(u > 0)
        if du > 0:
            terms.append(u < strips_count - 1)
        return functools.reduce(jnp.logical_and, terms)

    around = [(dt, du) for dt in (-1, 0, 1) for du in (-1, 0, 1) if (dt, du) != (0, 0)]

    def place(dt, du):
        return (dt + 1) * 3 + du + 1

    barrier = pltpu.get_barrier_semaphore()
    expected = jnp.int32(0)
    for dt, du in around:
        there = exists(dt, du)
        expected = expected + there.astype(jnp.int32)

        @pl.when(there)
        def _():
            pl.semaphore_signal(
                barrier, inc=1, device_id=(t + dt, u + du), device_id_type=pl.DeviceIdType.MESH
            )

    def message(phase, dt, du):
        adjoint = phase % 2
        if du == 0:
            s = (dt + 1) // 2
            if adjoint:
                src = z_send.at[phase // 2, s]
            else:
                src = est.at[pl.ds(top * s, HALO)]
            dst = z_recv.at[phase, 1 - s]
        elif dt == 0:
            s = (du + 1) // 2
            src = y_send.at[phase, s, pl.ds(PAD, side)]
            dst = y_recv.at[phase, 1 - s, pl.ds(PAD, side)]
        else:
            s, r = (dt + 1) // 2, (du + 1) // 2
            if adjoint:
                src = c_send.at[phase, 2 * s + r, pl.ds(8, 88)]
            else:
                src = y_send.at[phase, r, pl.ds(PAD + s * (side - 88), 88)]
            dst = c_recv.at[phase, 2 * (1 - s) + 1 - r, pl.ds(8, 88)]
        return pltpu.make_async_remote_copy(
            src_ref=src,
            dst_ref=dst,
            send_sem=send_sem.at[phase, place(dt, du)],
            recv_sem=recv_sem.at[phase, place(dt, du)],
            device_id=(t + dt, u + du),
            device_id_type=pl.DeviceIdType.MESH,
        )

    def send(phase, which):
        for dt, du in which:
            @pl.when(exists(dt, du))
            def _():
                message(phase, dt, du).start()

    def receive(phase, which):
        for dt, du in which:
            @pl.when(exists(-dt, -du))
            def _():
                message(phase, dt, du).wait_recv()

    def sent(phase, which):
        for dt, du in which:
            @pl.when(exists(dt, du))
            def _():
                message(phase, dt, du).wait_send()

    along_z = [(-1, 0), (1, 0)]
    along_y = [(0, -1), (0, 1)]
    corners = [(-1, -1), (-1, 1), (1, -1), (1, 1)]

    def pack(phase):
        def body(p, carry):
            y_send[phase, 0, pl.ds(PAD + HALO * p, HALO)] = est[p, 0:HALO]
            y_send[phase, 1, pl.ds(PAD + HALO * p, HALO)] = est[p, rows - HALO : rows]
            return carry

        lax.fori_loop(0, depth, body, 0)

    load_est.wait()
    pack(0)
    pl.semaphore_wait(barrier, expected)
    send(0, along_y + along_z + corners)

    def blank(n, carry):
        wide_in[pl.ds(pl.multiple_of(104 * n, 8), 104)] = jnp.zeros((104, lanes), f32)
        return carry

    lax.fori_loop(0, wide_in.shape[0] // 104, blank, 0)

    for phase in range(2 * ITERS):
        for s in range(2):
            y_recv[phase, s, 0:PAD] = jnp.zeros((PAD, lanes), f32)
            y_recv[phase, s, PAD + side : 2 * PAD + side] = jnp.zeros((PAD, lanes), f32)
            y_send[phase, s, 0:PAD] = jnp.zeros((PAD, lanes), f32)

            @pl.when(jnp.logical_not(exists(2 * s - 1, 0)))
            def _():
                z_recv[phase, s] = jnp.zeros((HALO, rows, lanes), f32)

            @pl.when(jnp.logical_not(exists(0, 2 * s - 1)))
            def _():
                y_recv[phase, s, PAD : PAD + side] = jnp.zeros((side, lanes), f32)

            for r in range(2):
                k = 2 * s + r
                c_recv[phase, k, 0:PAD] = jnp.zeros((PAD, lanes), f32)
                c_recv[phase, k, 96:104] = jnp.zeros((8, lanes), f32)
                c_send[phase, k, 80:104] = jnp.zeros((24, lanes), f32)

                @pl.when(jnp.logical_not(exists(2 * s - 1, 2 * r - 1)))
                def _():
                    c_recv[phase, k, 8:96] = jnp.zeros((88, lanes), f32)

    def weights_of(v, d):
        length = lengths[d, v]
        half = length // 2
        raw = []
        whole = jnp.float32(0)
        for j in range(TAPS):
            inside = j < length
            whole = whole + jnp.where(inside, taps[v, d, j], 0.0)
        scale = 1.0 / jnp.full((8, lanes), whole, f32)
        for j in range(TAPS):
            at = j - MID + half
            inside = jnp.logical_and(at >= 0, at < length)
            value = taps[v, d, jnp.clip(at, 0, TAPS - 1)]
            raw.append(jnp.where(inside, value, 0.0) * scale)
        return raw

    def filled(delta, raw):
        height, width = delta.shape
        parts = []
        for h in range(0, height, 8):
            row = []
            for w in range(0, width, 128):
                piece = delta[h : h + 8, w : w + 128]
                value = jnp.zeros(piece.shape, f32)
                for j in range(TAPS):
                    value = jnp.where(piece == j, raw[j], value)
                row.append(value)
            parts.append(jnp.concatenate(row, 1) if len(row) > 1 else row[0])
        return jnp.concatenate(parts, 0)

    def segmented(delta, seg, raw):
        high, low = split(filled(jnp.where(seg < 3, delta, FAR), raw))
        return jnp.where(seg < 2, high.astype(f32), low.astype(f32))

    sums = count * depth
    tall = -(-(rows + 2 * HALO) // 16) * 16
    zf_build[...] = jnp.zeros(zf_build.shape, f32)
    za_build[...] = jnp.zeros(za_build.shape, f32)

    free = depth - 2 * HALO
    bound = 2 * HALO
    split_at = count * free

    def planes_of(m):
        view = m // free
        rest = m - split_at
        late_view = rest // bound
        place = rest - late_view * bound
        late_own = jnp.where(place >= HALO, place + free, place)
        inner = m < split_at
        return jnp.where(inner, view, late_view), jnp.where(inner, HALO + m - view * free, late_own)

    def tables(v, carry):
        shift = offsets[0, v] + MID - 1
        raw = weights_of(v, 0)
        shape = zf_build.shape
        view, own = planes_of(iota(shape, 0))
        col = iota(shape, 1)
        seg = col // planes
        delta = col - seg * planes - own - shift
        zf_build[...] += segmented(jnp.where(view == v, delta, FAR), seg, raw)
        shape = za_build.shape
        col = iota(shape, 1)
        seg = col // sums
        view, own = planes_of(col - seg * sums)
        delta = iota(shape, 0) - own - shift
        za_build[...] += segmented(jnp.where(view == v, delta, FAR), seg, raw)
        raw = weights_of(v, 1)
        shift = offsets[1, v] + MID - 1
        shape = (rows, yf.shape[2])
        col = iota(shape, 1)
        seg = col // tall
        yf[v] = segmented(col - seg * tall - iota(shape, 0) - shift, seg, raw).astype(bf16)
        shape = (tall, ya.shape[2])
        col = iota(shape, 1)
        seg = col // rows
        ya[v] = segmented(iota(shape, 0) - (col - seg * rows) - shift, seg, raw).astype(bf16)
        raw = weights_of(v, 2)
        shift = offsets[2, v] - MID
        delta = iota((lanes, lanes), 0) - iota((lanes, lanes), 1)
        high, low = split(filled(delta - shift, raw))
        both = jnp.concatenate([high, low], 1)
        xf[v] = jnp.concatenate([both, both], 0)
        high, low = split(filled(-delta - shift, raw))
        both = jnp.concatenate([high, low], 1)
        xa[v] = jnp.concatenate([both, both], 0)
        return carry

    lax.fori_loop(0, count, tables, 0)
    zf[...] = zf_build[...].astype(bf16)
    za[...] = za_build[...].astype(bf16)

    def clear(n, carry):
        mid[pl.ds(pl.multiple_of(64 * n, 64), 64)] = jnp.zeros((64, lanes), f32)
        return carry

    lax.fori_loop(0, mid.shape[0] // 64, clear, 0)
    load_obs.wait()

    def tripled(x):
        a, b = split(x)
        return jnp.concatenate([a, b, a], 0)

    def gather_own():
        def body(p, carry):
            wide_in[pl.ds(pitch * (HALO + p) + HALO, rows)] = est[p]
            return carry

        lax.fori_loop(0, depth, body, 0)

    def gather_y(phase):
        def body(p, carry):
            for r in range(2):
                strip = y_recv[phase, r, pl.ds(PAD + HALO * p, HALO)]
                wide_in[pl.ds(pitch * (HALO + p) + (HALO + rows) * r, HALO)] = strip
            return carry

        lax.fori_loop(0, depth, body, 0)

    def gather_z(phase):
        def body(n, carry):
            for s in range(2):
                wide_in[pl.ds(pitch * (n + (HALO + depth) * s) + HALO, rows)] = z_recv[phase, s, n]
            return carry

        lax.fori_loop(0, HALO, body, 0)

    def gather_corners(phase):
        def body(n, carry):
            for s in range(2):
                at = pitch * (n + (HALO + depth) * s)
                for r in range(2):
                    start = PAD + HALO * n + (7 if s == 0 else 0)
                    strip = c_recv[phase, 2 * s + r, pl.ds(start, HALO)]
                    wide_in[pl.ds(at + (HALO + rows) * r, HALO)] = strip
            return carry

        lax.fori_loop(0, HALO, body, 0)

    def forward_z(ys, low, high):
        pair = [tripled(wide_in[pl.ds(y, planes, stride=pitch)]) for y in ys]
        table = zf[low : -(-high // 16) * 16, : 3 * planes]
        out = jnp.dot(table, jnp.concatenate(pair, 1), preferred_element_type=f32)
        for i, y in enumerate(ys):
            mid[pl.ds(low * pitch + y, high - low, stride=pitch)] = out[: high - low, i * lanes : (i + 1) * lanes]

    def own_rows(one_pair):
        def body(n, carry):
            for k in range(rows // 4):
                y = HALO + rows // 2 * n + 2 * k
                one_pair((y, y + 1))
            return carry

        lax.fori_loop(0, 2, body, 0)

    def rim_rows(one_pair):
        for k in range(HALO):
            one_pair((k, HALO + rows + k))

    first_row = u * rows
    inner_groups = [(v, free * v, list(range(HALO, top))) for v in range(count)]
    outer = list(range(HALO)) + list(range(top, depth))
    outer_groups = [(v, split_at + bound * v, outer) for v in range(count)]
    groups = inner_groups + outer_groups
    inner_low, inner_high = 0, -(-split_at // 8) * 8
    outer_low, outer_high = split_at // 16 * 16, sums

    def spread_rows(v, at, own):
        table = ya[v, :, : 3 * rows]
        for k in range(0, len(own), 2):
            pair = []
            for i in range(2):
                part = pl.ds((k + i) * rows, rows)
                a, b = gh[part], gl[part]
                pair.append(jnp.concatenate([a, b, a], 0))
            out = jnp.dot(table, jnp.concatenate(pair, 1), preferred_element_type=f32)
            for i in range(2):
                back_mid[pl.ds(pitch * (at + k + i), 72)] = out[:72, i * lanes : (i + 1) * lanes]

    def spread_lanes(v, at, own):
        used = pl.ds(0, len(own) * rows)
        out = jnp.dot(rb[used], xa[v], preferred_element_type=f32)
        gh[used], gl[used] = split(out[:, :lanes] + out[:, lanes:])

    def compare(v, at, own):
        place_y = first_row + iota((rows, lanes), 0)
        covered = jnp.logical_and(place_y >= field[0, v], place_y < field[1, v])
        back = level[v]
        out = jnp.dot(zb[pl.ds(0, len(own) * rows)], xf[v], preferred_element_type=f32)
        for k, p in enumerate(own):
            part = out[k * rows : (k + 1) * rows]
            blurred = part[:, :lanes] + part[:, lanes:]
            ratio = jnp.where(covered, obs[v, p] / (blurred + back), 1.0)
            rb[k * rows : (k + 1) * rows, :lanes], rb[k * rows : (k + 1) * rows, lanes:] = split(ratio)

    def blur_rows(v, at, own):
        table = yf[v, :, : 3 * tall]
        for k in range(0, len(own), 2):
            pair = [tripled(mid[pl.ds(pitch * (at + k + i), tall)]) for i in range(2)]
            out = jnp.dot(table, jnp.concatenate(pair, 1), preferred_element_type=f32)
            for i in range(2):
                part = pl.ds((k + i) * rows, rows)
                zb[part, :lanes], zb[part, lanes:] = split(out[:, i * lanes : (i + 1) * lanes])

    def trips(first, last):
        for n in range(first, last):
            for late_by, stage in ((3, spread_rows), (2, spread_lanes), (1, compare), (0, blur_rows)):
                if 0 <= n - late_by < len(groups):
                    stage(*groups[n - late_by])

    def inner_planes():
        trips(0, count)

    def outer_planes():
        trips(count, len(groups) + 3)

    def adjoint_z(ys):
        pair = [tripled(back_mid[pl.ds(y, sums, stride=pitch)]) for y in ys]
        out = jnp.dot(za[:, : 3 * sums], jnp.concatenate(pair, 1), preferred_element_type=f32)
        for i, y in enumerate(ys):
            wide_out[pl.ds(y, planes, stride=pitch)] = out[:, i * lanes : (i + 1) * lanes]

    def pack_outer(phase):
        def body(n, carry):
            for s in range(2):
                at = pitch * (n + (HALO + depth) * s)
                z_send[phase // 2, s, n] = wide_out[pl.ds(at + HALO, rows)]
            return carry

        lax.fori_loop(0, HALO, body, 0)

    def pack_corners(phase):
        def body(n, carry):
            for s in range(2):
                at = pitch * (n + (HALO + depth) * s)
                for r in range(2):
                    strip = wide_out[pl.ds(at + (HALO + rows) * r, HALO)]
                    c_send[phase, 2 * s + r, pl.ds(PAD + HALO * n, HALO)] = strip
            return carry

        lax.fori_loop(0, HALO, body, 0)

    def pack_inner(phase):
        def body(p, carry):
            for r in range(2):
                strip = wide_out[pl.ds(pitch * (HALO + p) + (HALO + rows) * r, HALO)]
                y_send[phase, r, pl.ds(PAD + HALO * p, HALO)] = strip
            return carry

        lax.fori_loop(0, depth, body, 0)

    early = iota((16, lanes), 0) < HALO
    late = iota((16, lanes), 0) >= 16 - HALO

    def update(phase, target):
        def plane(p, s, n):
            value = wide_out[pl.ds(pitch * (HALO + p) + HALO, rows)]
            head, body, tail = value[:16], value[16 : rows - 16], value[rows - 16 :]
            head = head + jnp.where(early, y_recv[phase, 0, pl.ds(PAD + HALO * p, 16)], 0.0)
            tail = tail + jnp.where(late, y_recv[phase, 1, pl.ds(1 + HALO * p, 16)], 0.0)
            if s is not None:
                head = head + jnp.where(early, c_recv[phase, 2 * s, pl.ds(PAD + HALO * n, 16)], 0.0)
                tail = tail + jnp.where(late, c_recv[phase, 2 * s + 1, pl.ds(1 + HALO * n, 16)], 0.0)
            value = jnp.concatenate([head, body, tail], 0)
            if s is not None:
                value = value + z_recv[phase, s, n]
            target[p] = est[p] * value * (1.0 / count)

        def low(n, carry):
            plane(n, 0, n)
            return carry

        def central(n, carry):
            plane(n, None, None)
            return carry

        def high(n, carry):
            plane(top + n, 1, n)
            return carry

        lax.fori_loop(0, HALO, low, 0)
        lax.fori_loop(HALO, top, central, 0)
        lax.fori_loop(0, HALO, high, 0)

    for step in range(ITERS):
        ahead, back = 2 * step, 2 * step + 1
        gather_own()
        receive(ahead, along_y)
        gather_y(ahead)
        own_rows(lambda ys: forward_z(ys, inner_low, inner_high))
        rim_rows(lambda ys: forward_z(ys, inner_low, inner_high))
        inner_planes()
        receive(ahead, along_z)
        gather_z(ahead)
        own_rows(lambda ys: forward_z(ys, outer_low, outer_high))
        receive(ahead, corners)
        gather_corners(ahead)
        rim_rows(lambda ys: forward_z(ys, outer_low, outer_high))
        outer_planes()
        own_rows(adjoint_z)
        pack_outer(back)
        send(back, along_z)
        rim_rows(adjoint_z)
        pack_inner(back)
        send(back, along_y)
        pack_corners(back)
        send(back, corners)
        receive(back, along_y + along_z + corners)
        sent(ahead, along_y + along_z + corners)
        if step < ITERS - 1:
            update(back, est)
            pack(ahead + 2)
            send(ahead + 2, along_y + along_z + corners)
        else:
            update(back, out_ref)
        sent(back, along_y + along_z + corners)


def solution(mesh):
    tiles, strips_count = mesh.shape["tile"], mesh.shape["view"]

    def on_device(estimate, views, background, psf_taps, psf_lengths, view_offsets, field_rows):
        count, depth, rows, lanes = views.shape
        reach = depth + 2 * HALO
        side = HALO * depth
        phases = 2 * ITERS
        pitch = rows + 2 * HALO + 1
        planes = -(-reach // 16) * 16
        tall = -(-(rows + 2 * HALO) // 16) * 16
        sums = count * depth
        anywhere = pl.BlockSpec(memory_space=pl.ANY)
        scalar = pl.BlockSpec(memory_space=pltpu.SMEM)
        v = pltpu.VMEM
        return pl.pallas_call(
            functools.partial(kernel, tiles, strips_count),
            out_shape=jax.ShapeDtypeStruct((depth, rows, lanes), f32),
            in_specs=[anywhere, anywhere] + [scalar] * 5,
            out_specs=pl.BlockSpec(memory_space=pltpu.VMEM),
            scratch_shapes=[
                v((depth, rows, lanes), f32),
                v((count, depth, rows, lanes), f32),
                v((planes * pitch + 8, lanes), f32),
                v((-(-(sums * pitch + 16) // 64) * 64, lanes), f32),
                v((sums * pitch + 16, lanes), f32),
                v((planes * pitch + 8, lanes), f32),
                v((sums, 256), f32),
                v((planes, 512), f32),
                v((sums, 256), bf16),
                v((planes, 512), bf16),
                v((count, rows, 256), bf16),
                v((count, tall, 256), bf16),
                v((count, 2 * lanes, 2 * lanes), bf16),
                v((count, 2 * lanes, 2 * lanes), bf16),
                v((2 * HALO * rows, 2 * lanes), bf16),
                v((2 * HALO * rows, 2 * lanes), bf16),
                v((2 * HALO * rows, lanes), bf16),
                v((2 * HALO * rows, lanes), bf16),
                v((ITERS, 2, HALO, rows, lanes), f32),
                v((phases, 2, side + 2 * PAD, lanes), f32),
                v((phases, 4, 104, lanes), f32),
                v((phases, 2, HALO, rows, lanes), f32),
                v((phases, 2, side + 2 * PAD, lanes), f32),
                v((phases, 4, 104, lanes), f32),
                pltpu.SemaphoreType.DMA((2,)),
                pltpu.SemaphoreType.DMA((phases, 9)),
                pltpu.SemaphoreType.DMA((phases, 9)),
            ],
            compiler_params=pltpu.CompilerParams(
                collective_id=0, has_side_effects=True, vmem_limit_bytes=60 * 2**20
            ),
            name="deconvolve",
        )(estimate, views, background, psf_taps, psf_lengths.T, view_offsets.T, field_rows.T)

    return jax.shard_map(
        on_device,
        mesh=mesh,
        in_specs=(P("tile", "view", None), P(None, "tile", "view", None), P(), P(), P(), P(), P()),
        out_specs=P("tile", "view", None),
        check_vma=False,
    )
```

```python
import functools

import jax
import jax.numpy as jnp
from jax import lax
from jax.experimental import pallas as pl
from jax.experimental.pallas import tpu as pltpu
from jax.sharding import PartitionSpec as P

ITERS = 2
HALO = 9
TAPS = 11
MID = 5
PAD = 8
FAR = 100000
STEP = 1000
f32 = jnp.float32
bf16 = jnp.bfloat16


def split(x):
    high = x.astype(bf16)
    low = (x - high.astype(f32)).astype(bf16)
    return high, low


def iota(shape, dim):
    return lax.broadcasted_iota(jnp.int32, shape, dim)


def kernel(
    tiles, strips_count,
    est_hbm, views_hbm, level, taps, lengths, offsets, field,
    out_ref,
    est, obs, wide_in, mid, back_mid, wide_out, zf_build, za_build, zf_code, za_code, yf_code, yf_seg, ya_code, ya_seg, zf, za, yf, ya, xf, xa,
    zb, rb, gh, gl,
    z_send, y_send, e_send, c_send, z_recv, y_recv, e_recv, c_recv,
    load_sem, send_sem, recv_sem,
):
    count, depth, rows, lanes = obs.shape
    reach = depth + 2 * HALO
    top = depth - HALO
    pitch = rows + 2 * HALO + 1
    planes = -(-reach // 16) * 16
    side = HALO * depth
    t = lax.axis_index("tile")
    u = lax.axis_index("view")

    load_est = pltpu.make_async_copy(est_hbm, est, load_sem.at[0])
    load_est.start()
    load_obs = pltpu.make_async_copy(views_hbm, obs, load_sem.at[1])
    load_obs.start()

    above = (t > 0, t < tiles - 1)
    beside = (u > 0, u < strips_count - 1)

    def at_z(s):
        return (t + 2 * s - 1, u)

    def at_y(r):
        return (t, u + 2 * r - 1)

    barrier = pltpu.get_barrier_semaphore()
    expected = jnp.int32(0)
    for there, where in [(above[s], at_z(s)) for s in range(2)] + [(beside[r], at_y(r)) for r in range(2)]:
        expected = expected + there.astype(jnp.int32)

        @pl.when(there)
        def _():
            pl.semaphore_signal(barrier, inc=1, device_id=where, device_id_type=pl.DeviceIdType.MESH)

    faces_z = [("z", s, None) for s in range(2)]
    edges = [("e", s, r) for s in range(2) for r in range(2)]
    faces_y = [("y", None, r) for r in range(2)]
    corners = [("c", s, r) for s in range(2) for r in range(2)]
    names = faces_z + edges + faces_y + corners
    inner = pl.ds(8, rows - 16)
    strip = pl.ds(PAD, 88)

    def message(phase, name):
        kind, s, r = name
        adjoint = phase % 2
        if kind == "z":
            src = z_send.at[phase // 2, s, :, inner] if adjoint else est.at[pl.ds(top * s, HALO), inner]
            dst, where = z_recv.at[phase, 1 - s, :, inner], at_z(s)
        elif kind == "y":
            src = y_send.at[phase, r, pl.ds(PAD, side)]
            dst, where = y_recv.at[phase, 1 - r, pl.ds(PAD, side)], at_y(r)
        elif kind == "e":
            if adjoint:
                src = e_send.at[phase // 2, 2 * s + r, strip]
            else:
                src = y_send.at[phase, r, pl.ds(PAD + s * (side - 88), 88)]
            dst, where = e_recv.at[phase, 2 * (1 - s) + r, strip], at_z(s)
        else:
            src = (c_send.at[phase // 2] if adjoint else e_recv.at[phase]).at[2 * s + r, strip]
            dst, where = c_recv.at[phase, 2 * s + 1 - r, strip], at_y(r)
        return pltpu.make_async_remote_copy(
            src_ref=src,
            dst_ref=dst,
            send_sem=send_sem.at[phase, names.index(name)],
            recv_sem=recv_sem.at[phase, names.index(name)],
            device_id=where,
            device_id_type=pl.DeviceIdType.MESH,
        )

    def outgoing(name):
        kind, s, r = name
        if kind == "y":
            return beside[r]
        return jnp.logical_and(above[s], beside[r]) if kind == "c" else above[s]

    def incoming(name):
        kind, s, r = name
        if kind == "y":
            return beside[1 - r]
        return jnp.logical_and(above[s], beside[1 - r]) if kind == "c" else above[1 - s]

    def send(phase, which):
        for name in which:
            @pl.when(outgoing(name))
            def _():
                message(phase, name).start()

    def receive(phase, which):
        for name in which:
            @pl.when(incoming(name))
            def _():
                message(phase, name).wait_recv()

    def sent(phase, which):
        for name in which:
            @pl.when(outgoing(name))
            def _():
                message(phase, name).wait_send()

    def pack(phase):
        def body(p, carry):
            y_send[phase, 0, pl.ds(PAD + HALO * p, HALO)] = est[p, 0:HALO]
            y_send[phase, 1, pl.ds(PAD + HALO * p, HALO)] = est[p, rows - HALO : rows]
            return carry

        lax.fori_loop(0, depth, body, 0)

    load_est.wait()
    pack(0)
    pl.semaphore_wait(barrier, expected)
    send(0, edges + faces_y + faces_z)

    def blank(n, carry):
        wide_in[pl.ds(pl.multiple_of(104 * n, 8), 104)] = jnp.zeros((104, lanes), f32)
        return carry

    lax.fori_loop(0, wide_in.shape[0] // 104, blank, 0)

    for phase in range(2 * ITERS):
        for s in range(2):
            y_recv[phase, s, 0:PAD] = jnp.zeros((PAD, lanes), f32)
            y_recv[phase, s, PAD + side : 2 * PAD + side] = jnp.zeros((PAD, lanes), f32)

            @pl.when(jnp.logical_not(above[s]))
            def _():
                z_recv[phase, s] = jnp.zeros((HALO, rows, lanes), f32)
                for r in range(2):
                    e_recv[phase, 2 * s + r, 8:96] = jnp.zeros((88, lanes), f32)

            @pl.when(jnp.logical_not(beside[s]))
            def _():
                y_recv[phase, s, PAD : PAD + side] = jnp.zeros((side, lanes), f32)

            for r in range(2):
                k = 2 * s + r
                for held in (e_recv, c_recv):
                    held[phase, k, 0:PAD] = jnp.zeros((PAD, lanes), f32)
                    held[phase, k, 96:104] = jnp.zeros((8, lanes), f32)

                @pl.when(jnp.logical_not(jnp.logical_and(above[s], beside[r])))
                def _():
                    c_recv[phase, k, 8:96] = jnp.zeros((88, lanes), f32)

    def weights_of(v, d):
        length = lengths[d, v]
        half = length // 2
        raw = []
        whole = jnp.float32(0)
        for j in range(TAPS):
            inside = j < length
            whole = whole + jnp.where(inside, taps[v, d, j], 0.0)
        scale = 1.0 / jnp.full((8, lanes), whole, f32)
        for j in range(TAPS):
            at = j - MID + half
            inside = jnp.logical_and(at >= 0, at < length)
            value = taps[v, d, jnp.clip(at, 0, TAPS - 1)]
            raw.append(jnp.where(inside, value, 0.0) * scale)
        return raw

    def filled(delta, raw):
        height, width = delta.shape
        parts = []
        for h in range(0, height, 8):
            row = []
            for w in range(0, width, 128):
                piece = delta[h : h + 8, w : w + 128]
                value = jnp.zeros(piece.shape, f32)
                for j in range(TAPS):
                    value = jnp.where(piece == j, raw[j], value)
                row.append(value)
            parts.append(jnp.concatenate(row, 1) if len(row) > 1 else row[0])
        return jnp.concatenate(parts, 0)

    def in_segments(value, seg):
        high, low = split(value)
        return jnp.where(seg < 2, high.astype(f32), low.astype(f32)).astype(bf16)

    sums = count * depth
    tall = -(-(rows + 2 * HALO) // 16) * 16
    zf_build[...] = jnp.zeros(zf_build.shape, f32)
    za_build[...] = jnp.zeros(za_build.shape, f32)

    free = depth - 2 * HALO
    bound = 2 * HALO
    split_at = count * free

    def planes_of(m):
        view = m // free
        rest = m - split_at
        late_view = rest // bound
        place = rest - late_view * bound
        late_own = jnp.where(place >= HALO, place + free, place)
        inner = m < split_at
        return jnp.where(inner, view, late_view), jnp.where(inner, HALO + m - view * free, late_own)

    view, own = planes_of(iota(zf_code.shape, 0))
    col = iota(zf_code.shape, 1)
    zf_seg = col // planes
    zf_code[...] = jnp.where(zf_seg < 3, col - zf_seg * planes - own + STEP * view, FAR)
    view, own = planes_of(iota(za_code.shape, 1))
    za_code[...] = iota(za_code.shape, 0) - own + STEP * view
    col = iota(yf_code.shape, 1)
    yf_seg[...] = col // tall
    yf_code[...] = jnp.where(yf_seg[...] < 3, col - yf_seg[...] * tall - iota(yf_code.shape, 0), FAR)
    col = iota(ya_code.shape, 1)
    ya_seg[...] = col // rows
    ya_code[...] = jnp.where(ya_seg[...] < 3, iota(ya_code.shape, 0) - (col - ya_seg[...] * rows), FAR)

    def tables(v, carry):
        shift = offsets[0, v] + MID - 1
        raw = weights_of(v, 0)
        zf_build[...] += filled(zf_code[...] - (shift + STEP * v), raw)
        za_build[...] += filled(za_code[...] - (shift + STEP * v), raw)
        raw = weights_of(v, 1)
        shift = offsets[1, v] + MID - 1
        yf[v] = in_segments(filled(yf_code[...] - shift, raw), yf_seg[...])
        ya[v] = in_segments(filled(ya_code[...] - shift, raw), ya_seg[...])
        raw = weights_of(v, 2)
        shift = offsets[2, v] - MID
        delta = iota((lanes, lanes), 0) - iota((lanes, lanes), 1)
        high, low = split(filled(delta - shift, raw))
        both = jnp.concatenate([high, low], 1)
        xf[v] = jnp.concatenate([both, both], 0)
        high, low = split(filled(-delta - shift, raw))
        both = jnp.concatenate([high, low], 1)
        xa[v] = jnp.concatenate([both, both], 0)
        return carry

    lax.fori_loop(0, count // 2, tables, 0)
    receive(0, edges)
    send(0, corners)
    lax.fori_loop(count // 2, count, tables, 0)
    zf[...] = in_segments(zf_build[...], zf_seg)
    za[:planes], za[planes:] = split(za_build[...])

    def clear(n, carry):
        mid[pl.ds(pl.multiple_of(64 * n, 64), 64)] = jnp.zeros((64, lanes), f32)
        return carry

    lax.fori_loop(0, mid.shape[0] // 64, clear, 0)
    load_obs.wait()

    def tripled(x):
        a, b = split(x)
        return jnp.concatenate([a, b, a], 0)

    def gather_own():
        def body(p, carry):
            wide_in[pl.ds(pitch * (HALO + p) + HALO, rows)] = est[p]
            return carry

        lax.fori_loop(0, depth, body, 0)

    def gather_y(phase):
        def body(p, carry):
            for r in range(2):
                strip = y_recv[phase, r, pl.ds(PAD + HALO * p, HALO)]
                wide_in[pl.ds(pitch * (HALO + p) + (HALO + rows) * r, HALO)] = strip
            return carry

        lax.fori_loop(0, depth, body, 0)

    def gather_z(phase):
        def body(n, carry):
            for s in range(2):
                at = pitch * (n + (HALO + depth) * s) + HALO
                start = PAD + HALO * n + (7 if s == 0 else 0)
                wide_in[pl.ds(at + 8, rows - 16)] = z_recv[phase, s, n, inner]
                for r in range(2):
                    wide_in[pl.ds(at + (rows - HALO) * r, HALO)] = e_recv[phase, 2 * s + r, pl.ds(start, HALO)]
            return carry

        lax.fori_loop(0, HALO, body, 0)

    def gather_corners(phase):
        def body(n, carry):
            for s in range(2):
                at = pitch * (n + (HALO + depth) * s)
                start = PAD + HALO * n + (7 if s == 0 else 0)
                for r in range(2):
                    strip = c_recv[phase, 2 * s + r, pl.ds(start, HALO)]
                    wide_in[pl.ds(at + (HALO + rows) * r, HALO)] = strip
            return carry

        lax.fori_loop(0, HALO, body, 0)

    def forward_z(ys, low, high):
        pair = [tripled(wide_in[pl.ds(y, planes, stride=pitch)]) for y in ys]
        table = zf[low : -(-high // 16) * 16, : 3 * planes]
        out = jnp.dot(table, jnp.concatenate(pair, 1), preferred_element_type=f32)
        for i, y in enumerate(ys):
            mid[pl.ds(low * pitch + y, high - low, stride=pitch)] = out[: high - low, i * lanes : (i + 1) * lanes]

    def own_rows(one_pair):
        def body(n, carry):
            for k in range(rows // 4):
                y = HALO + rows // 2 * n + 2 * k
                one_pair((y, y + 1))
            return carry

        lax.fori_loop(0, 2, body, 0)

    def rim_rows(one_pair):
        for k in range(HALO):
            one_pair((k, HALO + rows + k))

    first_row = u * rows
    inner_groups = [(v, free * v, list(range(HALO, top))) for v in range(count)]
    outer = list(range(HALO)) + list(range(top, depth))
    outer_groups = [(v, split_at + bound * v, outer) for v in range(count)]
    groups = inner_groups + outer_groups
    inner_low, inner_high = 0, -(-split_at // 8) * 8
    outer_low, outer_high = split_at // 16 * 16, sums

    def spread_rows(v, at, own):
        table = ya[v, :, : 3 * rows]
        for k in range(0, len(own), 2):
            pair = []
            for i in range(2):
                part = pl.ds((k + i) * rows, rows)
                a, b = gh[part], gl[part]
                pair.append(jnp.concatenate([a, b, a], 0))
            out = jnp.dot(table, jnp.concatenate(pair, 1), preferred_element_type=f32)
            for i in range(2):
                back_mid[pl.ds(pitch * (at + k + i), 72)] = out[:72, i * lanes : (i + 1) * lanes]

    def spread_lanes(v, at, own):
        used = pl.ds(0, len(own) * rows)
        out = jnp.dot(rb[used], xa[v], preferred_element_type=f32)
        gh[used], gl[used] = split(out[:, :lanes] + out[:, lanes:])

    def compare(v, at, own):
        place_y = first_row + iota((rows, lanes), 0)
        covered = jnp.logical_and(place_y >= field[0, v], place_y < field[1, v])
        back = level[v]
        out = jnp.dot(zb[pl.ds(0, len(own) * rows)], xf[v], preferred_element_type=f32)
        for k, p in enumerate(own):
            part = out[k * rows : (k + 1) * rows]
            blurred = part[:, :lanes] + part[:, lanes:]
            ratio = jnp.where(covered, obs[v, p] / (blurred + back), 1.0)
            rb[k * rows : (k + 1) * rows, :lanes], rb[k * rows : (k + 1) * rows, lanes:] = split(ratio)

    def blur_rows(v, at, own):
        table = yf[v, :, : 3 * tall]
        for k in range(0, len(own), 2):
            pair = [tripled(mid[pl.ds(pitch * (at + k + i), tall)]) for i in range(2)]
            out = jnp.dot(table, jnp.concatenate(pair, 1), preferred_element_type=f32)
            for i in range(2):
                part = pl.ds((k + i) * rows, rows)
                zb[part, :lanes], zb[part, lanes:] = split(out[:, i * lanes : (i + 1) * lanes])

    def trips(first, last):
        for n in range(first, last):
            for late_by, stage in ((3, spread_rows), (2, spread_lanes), (1, compare), (0, blur_rows)):
                if 0 <= n - late_by < len(groups):
                    stage(*groups[n - late_by])

    def inner_planes():
        trips(0, count)

    def outer_planes():
        trips(count, len(groups) + 3)

    def adjoint_z(ys):
        pair = [split(back_mid[pl.ds(y, sums, stride=pitch)]) for y in ys]
        high, low = (jnp.concatenate(part, 1) for part in zip(*pair))
        out = jnp.dot(za[:, :sums], high, preferred_element_type=f32)
        out = out[:planes] + out[planes:]
        out = out + jnp.dot(za[:planes, :sums], low, preferred_element_type=f32)
        for i, y in enumerate(ys):
            wide_out[pl.ds(y, planes, stride=pitch)] = out[:, i * lanes : (i + 1) * lanes]

    def pack_outer(step):
        def body(n, carry):
            for s in range(2):
                at = pitch * (n + (HALO + depth) * s)
                z_send[step, s, n, inner] = wide_out[pl.ds(at + HALO + 8, rows - 16)]
            return carry

        lax.fori_loop(0, HALO, body, 0)

    def pack_corners(step):
        def body(n, carry):
            for s in range(2):
                at = pitch * (n + (HALO + depth) * s)
                for r in range(2):
                    part = wide_out[pl.ds(at + (HALO + rows) * r, HALO)]
                    c_send[step, 2 * s + r, pl.ds(PAD + HALO * n, HALO)] = part
            return carry

        lax.fori_loop(0, HALO, body, 0)

    def pack_edges(phase):
        def body(n, carry):
            for s in range(2):
                for r in range(2):
                    at = pitch * (n + (HALO + depth) * s) + HALO + (rows - HALO) * r
                    part = wide_out[pl.ds(at, HALO)] + c_recv[phase, 2 * s + r, pl.ds(PAD + HALO * n, HALO)]
                    e_send[phase // 2, 2 * s + r, pl.ds(PAD + HALO * n, HALO)] = part
            return carry

        lax.fori_loop(0, HALO, body, 0)

    def pack_inner(phase):
        def body(p, carry):
            for r in range(2):
                strip = wide_out[pl.ds(pitch * (HALO + p) + (HALO + rows) * r, HALO)]
                y_send[phase, r, pl.ds(PAD + HALO * p, HALO)] = strip
            return carry

        lax.fori_loop(0, depth, body, 0)

    early = iota((16, lanes), 0) < HALO
    late = iota((16, lanes), 0) >= 16 - HALO

    def update(phase, target):
        def plane(p, s, n):
            value = wide_out[pl.ds(pitch * (HALO + p) + HALO, rows)]
            head, body, tail = value[:16], value[16 : rows - 16], value[rows - 16 :]
            first = y_recv[phase, 0, pl.ds(PAD + HALO * p, 16)]
            last = y_recv[phase, 1, pl.ds(1 + HALO * p, 16)]
            if s is not None:
                first = first + e_recv[phase, 2 * s, pl.ds(PAD + HALO * n, 16)]
                last = last + e_recv[phase, 2 * s + 1, pl.ds(1 + HALO * n, 16)]
                near = z_recv[phase, s, n]
                first = jnp.where(early, first, near[:16])
                last = jnp.where(late, last, near[rows - 16 :])
                body = body + near[16 : rows - 16]
            else:
                first = jnp.where(early, first, 0.0)
                last = jnp.where(late, last, 0.0)
            value = jnp.concatenate([head + first, body, tail + last], 0)
            target[p] = est[p] * value * (1.0 / count)

        def low(n, carry):
            plane(n, 0, n)
            return carry

        def central(n, carry):
            plane(n, None, None)
            return carry

        def high(n, carry):
            plane(top + n, 1, n)
            return carry

        lax.fori_loop(0, HALO, low, 0)
        lax.fori_loop(HALO, top, central, 0)
        lax.fori_loop(0, HALO, high, 0)

    for step in range(ITERS):
        ahead, back = 2 * step, 2 * step + 1
        gather_own()
        own_rows(lambda ys: forward_z(ys, inner_low, inner_high))
        if step > 0:
            receive(ahead, edges)
            send(ahead, corners)
        receive(ahead, faces_y)
        gather_y(ahead)
        rim_rows(lambda ys: forward_z(ys, inner_low, inner_high))
        inner_planes()
        receive(ahead, faces_z)
        gather_z(ahead)
        own_rows(lambda ys: forward_z(ys, outer_low, outer_high))
        receive(ahead, corners)
        gather_corners(ahead)
        rim_rows(lambda ys: forward_z(ys, outer_low, outer_high))
        outer_planes()
        rim_rows(adjoint_z)
        pack_corners(step)
        send(back, corners)
        own_rows(adjoint_z)
        pack_outer(step)
        send(back, faces_z)
        pack_inner(back)
        send(back, faces_y)
        receive(back, corners)
        pack_edges(back)
        send(back, edges)
        receive(back, faces_y + faces_z + edges)
        sent(ahead, names)
        if step < ITERS - 1:
            update(back, est)
            pack(ahead + 2)
            send(ahead + 2, edges + faces_y + faces_z)
        else:
            update(back, out_ref)
        sent(back, names)


def solution(mesh):
    tiles, strips_count = mesh.shape["tile"], mesh.shape["view"]

    def on_device(estimate, views, background, psf_taps, psf_lengths, view_offsets, field_rows):
        count, depth, rows, lanes = views.shape
        reach = depth + 2 * HALO
        side = HALO * depth
        phases = 2 * ITERS
        pitch = rows + 2 * HALO + 1
        planes = -(-reach // 16) * 16
        tall = -(-(rows + 2 * HALO) // 16) * 16
        sums = count * depth
        anywhere = pl.BlockSpec(memory_space=pl.ANY)
        scalar = pl.BlockSpec(memory_space=pltpu.SMEM)
        v = pltpu.VMEM
        return pl.pallas_call(
            functools.partial(kernel, tiles, strips_count),
            out_shape=jax.ShapeDtypeStruct((depth, rows, lanes), f32),
            in_specs=[anywhere, anywhere] + [scalar] * 5,
            out_specs=pl.BlockSpec(memory_space=pltpu.VMEM),
            scratch_shapes=[
                v((depth, rows, lanes), f32),
                v((count, depth, rows, lanes), f32),
                v((planes * pitch + 8, lanes), f32),
                v((-(-(sums * pitch + 16) // 64) * 64, lanes), f32),
                v((sums * pitch + 16, lanes), f32),
                v((planes * pitch + 8, lanes), f32),
                v((sums, 256), f32),
                v((planes, 256), f32),
                v((sums, 256), jnp.int32),
                v((planes, 256), jnp.int32),
                v((rows, 256), jnp.int32),
                v((rows, 256), jnp.int32),
                v((tall, 256), jnp.int32),
                v((tall, 256), jnp.int32),
                v((sums, 256), bf16),
                v((2 * planes, 256), bf16),
                v((count, rows, 256), bf16),
                v((count, tall, 256), bf16),
                v((count, 2 * lanes, 2 * lanes), bf16),
                v((count, 2 * lanes, 2 * lanes), bf16),
                v((2 * HALO * rows, 2 * lanes), bf16),
                v((2 * HALO * rows, 2 * lanes), bf16),
                v((2 * HALO * rows, lanes), bf16),
                v((2 * HALO * rows, lanes), bf16),
                v((ITERS, 2, HALO, rows, lanes), f32),
                v((phases, 2, side + 2 * PAD, lanes), f32),
                v((ITERS, 4, 104, lanes), f32),
                v((ITERS, 4, 104, lanes), f32),
                v((phases, 2, HALO, rows, lanes), f32),
                v((phases, 2, side + 2 * PAD, lanes), f32),
                v((phases, 4, 104, lanes), f32),
                v((phases, 4, 104, lanes), f32),
                pltpu.SemaphoreType.DMA((2,)),
                pltpu.SemaphoreType.DMA((phases, 12)),
                pltpu.SemaphoreType.DMA((phases, 12)),
            ],
            compiler_params=pltpu.CompilerParams(
                collective_id=0, has_side_effects=True, vmem_limit_bytes=60 * 2**20
            ),
            name="deconvolve",
        )(estimate, views, background, psf_taps, psf_lengths.T, view_offsets.T, field_rows.T)

    return jax.shard_map(
        on_device,
        mesh=mesh,
        in_specs=(P("tile", "view", None), P(None, "tile", "view", None), P(), P(), P(), P(), P()),
        out_specs=P("tile", "view", None),
        check_vma=False,
    )
```

```python
import functools

import jax
import jax.numpy as jnp
from jax import lax
from jax.experimental import pallas as pl
from jax.experimental.pallas import tpu as pltpu
from jax.sharding import PartitionSpec as P

ITERS = 2
HALO = 9
TAPS = 11
MID = 5
PAD = 8
FAR = 100000
STEP = 1000
f32 = jnp.float32
bf16 = jnp.bfloat16


def split(x):
    high = x.astype(bf16)
    low = (x - high.astype(f32)).astype(bf16)
    return high, low


def iota(shape, dim):
    return lax.broadcasted_iota(jnp.int32, shape, dim)


def kernel(
    tiles, strips_count,
    est_hbm, views_hbm, level, taps, lengths, offsets, field,
    out_ref,
    est, obs, wide_in, mid, back_mid, wide_out, zf_build, za_build, zf_code, za_code, yf_code, yf_seg, ya_code, ya_seg, zf, za, yf, ya, xf, xa,
    zb, rb, gh, gl,
    z_send, y_send, e_send, c_send, z_recv, y_recv, e_recv, c_recv,
    load_sem, send_sem, recv_sem,
):
    count, depth, rows, lanes = obs.shape
    reach = depth + 2 * HALO
    top = depth - HALO
    pitch = rows + 2 * HALO + 1
    planes = -(-reach // 16) * 16
    side = HALO * depth
    t = lax.axis_index("tile")
    u = lax.axis_index("view")

    load_est = pltpu.make_async_copy(est_hbm, est, load_sem.at[0])
    load_est.start()
    load_obs = pltpu.make_async_copy(views_hbm, obs, load_sem.at[1])
    load_obs.start()

    above = (t > 0, t < tiles - 1)
    beside = (u > 0, u < strips_count - 1)

    def at_z(s):
        return (t + 2 * s - 1, u)

    def at_y(r):
        return (t, u + 2 * r - 1)

    barrier = pltpu.get_barrier_semaphore()
    expected = jnp.int32(0)
    for there, where in [(above[s], at_z(s)) for s in range(2)] + [(beside[r], at_y(r)) for r in range(2)]:
        expected = expected + there.astype(jnp.int32)

        @pl.when(there)
        def _():
            pl.semaphore_signal(barrier, inc=1, device_id=where, device_id_type=pl.DeviceIdType.MESH)

    faces_z = [("z", s, None) for s in range(2)]
    edges = [("e", s, r) for s in range(2) for r in range(2)]
    faces_y = [("y", None, r) for r in range(2)]
    corners = [("c", s, r) for s in range(2) for r in range(2)]
    names = faces_z + edges + faces_y + corners
    inner = pl.ds(8, rows - 16)
    strip = pl.ds(PAD, 88)

    def message(phase, name):
        kind, s, r = name
        adjoint = phase % 2
        if kind == "z":
            src = z_send.at[phase // 2, s, :, inner] if adjoint else est.at[pl.ds(top * s, HALO), inner]
            dst, where = z_recv.at[phase, 1 - s, :, inner], at_z(s)
        elif kind == "y":
            src = y_send.at[phase, r, pl.ds(PAD, side)]
            dst, where = y_recv.at[phase, 1 - r, pl.ds(PAD, side)], at_y(r)
        elif kind == "e":
            if adjoint:
                src = e_send.at[phase // 2, 2 * s + r, strip]
            else:
                src = y_send.at[phase, r, pl.ds(PAD + s * (side - 88), 88)]
            dst, where = e_recv.at[phase, 2 * (1 - s) + r, strip], at_z(s)
        else:
            src = (c_send.at[phase // 2] if adjoint else e_recv.at[phase]).at[2 * s + r, strip]
            dst, where = c_recv.at[phase, 2 * s + 1 - r, strip], at_y(r)
        return pltpu.make_async_remote_copy(
            src_ref=src,
            dst_ref=dst,
            send_sem=send_sem.at[phase, names.index(name)],
            recv_sem=recv_sem.at[phase, names.index(name)],
            device_id=where,
            device_id_type=pl.DeviceIdType.MESH,
        )

    def outgoing(name):
        kind, s, r = name
        if kind == "y":
            return beside[r]
        return jnp.logical_and(above[s], beside[r]) if kind == "c" else above[s]

    def incoming(name):
        kind, s, r = name
        if kind == "y":
            return beside[1 - r]
        return jnp.logical_and(above[s], beside[1 - r]) if kind == "c" else above[1 - s]

    def send(phase, which):
        for name in which:
            @pl.when(outgoing(name))
            def _():
                message(phase, name).start()

    def receive(phase, which):
        for name in which:
            @pl.when(incoming(name))
            def _():
                message(phase, name).wait_recv()

    def sent(phase, which):
        for name in which:
            @pl.when(outgoing(name))
            def _():
                message(phase, name).wait_send()

    def pack(phase):
        def body(p, carry):
            y_send[phase, 0, pl.ds(PAD + HALO * p, HALO)] = est[p, 0:HALO]
            y_send[phase, 1, pl.ds(PAD + HALO * p, HALO)] = est[p, rows - HALO : rows]
            return carry

        lax.fori_loop(0, depth, body, 0)

    load_est.wait()
    pack(0)
    pl.semaphore_wait(barrier, expected)
    send(0, edges + faces_y + faces_z)

    def blank(n, carry):
        wide_in[pl.ds(pl.multiple_of(104 * n, 8), 104)] = jnp.zeros((104, lanes), f32)
        return carry

    lax.fori_loop(0, wide_in.shape[0] // 104, blank, 0)

    for phase in range(2 * ITERS):
        for s in range(2):
            y_recv[phase, s, 0:PAD] = jnp.zeros((PAD, lanes), f32)
            y_recv[phase, s, PAD + side : 2 * PAD + side] = jnp.zeros((PAD, lanes), f32)

            @pl.when(jnp.logical_not(above[s]))
            def _():
                z_recv[phase, s] = jnp.zeros((HALO, rows, lanes), f32)
                for r in range(2):
                    e_recv[phase, 2 * s + r, 8:96] = jnp.zeros((88, lanes), f32)

            @pl.when(jnp.logical_not(beside[s]))
            def _():
                y_recv[phase, s, PAD : PAD + side] = jnp.zeros((side, lanes), f32)

            for r in range(2):
                k = 2 * s + r
                for held in (e_recv, c_recv):
                    held[phase, k, 0:PAD] = jnp.zeros((PAD, lanes), f32)
                    held[phase, k, 96:104] = jnp.zeros((8, lanes), f32)

                @pl.when(jnp.logical_not(jnp.logical_and(above[s], beside[r])))
                def _():
                    c_recv[phase, k, 8:96] = jnp.zeros((88, lanes), f32)

    def weights_of(v, d):
        length = lengths[d, v]
        half = length // 2
        raw = []
        whole = jnp.float32(0)
        for j in range(TAPS):
            inside = j < length
            whole = whole + jnp.where(inside, taps[v, d, j], 0.0)
        scale = 1.0 / jnp.full((8, lanes), whole, f32)
        for j in range(TAPS):
            at = j - MID + half
            inside = jnp.logical_and(at >= 0, at < length)
            value = taps[v, d, jnp.clip(at, 0, TAPS - 1)]
            raw.append(jnp.where(inside, value, 0.0) * scale)
        return raw

    def filled(delta, raw):
        height, width = delta.shape
        parts = []
        for h in range(0, height, 8):
            row = []
            for w in range(0, width, 128):
                piece = delta[h : h + 8, w : w + 128]
                value = jnp.zeros(piece.shape, f32)
                for j in range(TAPS):
                    value = jnp.where(piece == j, raw[j], value)
                row.append(value)
            parts.append(jnp.concatenate(row, 1) if len(row) > 1 else row[0])
        return jnp.concatenate(parts, 0)

    def in_segments(value, seg):
        high, low = split(value)
        return jnp.where(seg < 2, high.astype(f32), low.astype(f32)).astype(bf16)

    sums = count * depth
    tall = -(-(rows + 2 * HALO) // 16) * 16
    zf_build[...] = jnp.zeros(zf_build.shape, f32)
    za_build[...] = jnp.zeros(za_build.shape, f32)

    free = depth - 2 * HALO
    bound = 2 * HALO
    split_at = count * free

    def planes_of(m):
        view = m // free
        rest = m - split_at
        late_view = rest // bound
        place = rest - late_view * bound
        late_own = jnp.where(place >= HALO, place + free, place)
        inner = m < split_at
        return jnp.where(inner, view, late_view), jnp.where(inner, HALO + m - view * free, late_own)

    view, own = planes_of(iota(zf_code.shape, 0))
    col = iota(zf_code.shape, 1)
    zf_seg = col // planes
    zf_code[...] = jnp.where(zf_seg < 3, col - zf_seg * planes - own + STEP * view, FAR)
    view, own = planes_of(iota(za_code.shape, 1))
    za_code[...] = iota(za_code.shape, 0) - own + STEP * view
    col = iota(yf_code.shape, 1)
    yf_seg[...] = col // tall
    yf_code[...] = jnp.where(yf_seg[...] < 3, col - yf_seg[...] * tall - iota(yf_code.shape, 0), FAR)
    col = iota(ya_code.shape, 1)
    ya_seg[...] = col // rows
    ya_code[...] = jnp.where(ya_seg[...] < 3, iota(ya_code.shape, 0) - (col - ya_seg[...] * rows), FAR)

    def tables(v, carry):
        shift = offsets[0, v] + MID - 1
        raw = weights_of(v, 0)
        zf_build[...] += filled(zf_code[...] - (shift + STEP * v), raw)
        za_build[...] += filled(za_code[...] - (shift + STEP * v), raw)
        raw = weights_of(v, 1)
        shift = offsets[1, v] + MID - 1
        yf[v] = in_segments(filled(yf_code[...] - shift, raw), yf_seg[...])
        ya[v] = in_segments(filled(ya_code[...] - shift, raw), ya_seg[...])
        raw = weights_of(v, 2)
        shift = offsets[2, v] - MID
        delta = iota((lanes, lanes), 0) - iota((lanes, lanes), 1)
        high, low = split(filled(delta - shift, raw))
        both = jnp.concatenate([high, low], 1)
        xf[v] = jnp.concatenate([both, both], 0)
        high, low = split(filled(-delta - shift, raw))
        both = jnp.concatenate([high, low], 1)
        xa[v] = jnp.concatenate([both, both], 0)
        return carry

    lax.fori_loop(0, count // 2, tables, 0)
    receive(0, edges)
    send(0, corners)
    lax.fori_loop(count // 2, count, tables, 0)
    zf[...] = in_segments(zf_build[...], zf_seg)
    za[:planes], za[planes:] = split(za_build[...])

    def clear(n, carry):
        mid[pl.ds(pl.multiple_of(64 * n, 64), 64)] = jnp.zeros((64, lanes), f32)
        return carry

    lax.fori_loop(0, mid.shape[0] // 64, clear, 0)
    load_obs.wait()

    def tripled(x):
        a, b = split(x)
        return jnp.concatenate([a, b, a], 0)

    def gather_own():
        def body(p, carry):
            wide_in[pl.ds(pitch * (HALO + p) + HALO, rows)] = est[p]
            return carry

        lax.fori_loop(0, depth, body, 0)

    def gather_y(phase):
        def body(p, carry):
            for r in range(2):
                strip = y_recv[phase, r, pl.ds(PAD + HALO * p, HALO)]
                wide_in[pl.ds(pitch * (HALO + p) + (HALO + rows) * r, HALO)] = strip
            return carry

        lax.fori_loop(0, depth, body, 0)

    def gather_z(phase):
        def body(n, carry):
            for s in range(2):
                at = pitch * (n + (HALO + depth) * s) + HALO
                start = PAD + HALO * n + (7 if s == 0 else 0)
                wide_in[pl.ds(at + 8, rows - 16)] = z_recv[phase, s, n, inner]
                for r in range(2):
                    wide_in[pl.ds(at + (rows - HALO) * r, HALO)] = e_recv[phase, 2 * s + r, pl.ds(start, HALO)]
            return carry

        lax.fori_loop(0, HALO, body, 0)

    def gather_corners(phase):
        def body(n, carry):
            for s in range(2):
                at = pitch * (n + (HALO + depth) * s)
                start = PAD + HALO * n + (7 if s == 0 else 0)
                for r in range(2):
                    strip = c_recv[phase, 2 * s + r, pl.ds(start, HALO)]
                    wide_in[pl.ds(at + (HALO + rows) * r, HALO)] = strip
            return carry

        lax.fori_loop(0, HALO, body, 0)

    def forward_z(ys, low, high):
        pair = [tripled(wide_in[pl.ds(y, planes, stride=pitch)]) for y in ys]
        table = zf[low : -(-high // 16) * 16, : 3 * planes]
        out = jnp.dot(table, jnp.concatenate(pair, 1), preferred_element_type=f32)
        for i, y in enumerate(ys):
            mid[pl.ds(low * pitch + y, high - low, stride=pitch)] = out[: high - low, i * lanes : (i + 1) * lanes]

    def own_rows(one_pair):
        def body(n, carry):
            for k in range(rows // 4):
                y = HALO + rows // 2 * n + 2 * k
                one_pair((y, y + 1))
            return carry

        lax.fori_loop(0, 2, body, 0)

    def rim_rows(one_pair):
        for k in range(HALO):
            one_pair((k, HALO + rows + k))

    first_row = u * rows
    inner_groups = [(v, free * v, list(range(HALO, top))) for v in range(count)]
    outer = list(range(HALO)) + list(range(top, depth))
    outer_groups = [(v, split_at + bound * v, outer) for v in range(count)]
    groups = inner_groups + outer_groups
    inner_low, inner_high = 0, -(-split_at // 8) * 8
    outer_low, outer_high = split_at // 16 * 16, sums

    def spread_rows(v, at, own):
        table = ya[v, :, : 3 * rows]
        for k in range(0, len(own), 2):
            pair = []
            for i in range(2):
                part = pl.ds((k + i) * rows, rows)
                a, b = gh[part], gl[part]
                pair.append(jnp.concatenate([a, b, a], 0))
            out = jnp.dot(table, jnp.concatenate(pair, 1), preferred_element_type=f32)
            for i in range(2):
                back_mid[pl.ds(pitch * (at + k + i), 72)] = out[:72, i * lanes : (i + 1) * lanes]

    def spread_lanes(v, at, own):
        used = pl.ds(0, len(own) * rows)
        out = jnp.dot(rb[used], xa[v], preferred_element_type=f32)
        gh[used], gl[used] = split(out[:, :lanes] + out[:, lanes:])

    def compare(v, at, own):
        place_y = first_row + iota((rows, lanes), 0)
        covered = jnp.logical_and(place_y >= field[0, v], place_y < field[1, v])
        back = level[v]
        out = jnp.dot(zb[pl.ds(0, len(own) * rows)], xf[v], preferred_element_type=f32)
        for k, p in enumerate(own):
            part = out[k * rows : (k + 1) * rows]
            blurred = part[:, :lanes] + part[:, lanes:]
            ratio = jnp.where(covered, obs[v, p] / (blurred + back), 1.0)
            rb[k * rows : (k + 1) * rows, :lanes], rb[k * rows : (k + 1) * rows, lanes:] = split(ratio)

    def blur_rows(v, at, own):
        table = yf[v, :, : 3 * tall]
        for k in range(0, len(own), 2):
            pair = [tripled(mid[pl.ds(pitch * (at + k + i), tall)]) for i in range(2)]
            out = jnp.dot(table, jnp.concatenate(pair, 1), preferred_element_type=f32)
            for i in range(2):
                part = pl.ds((k + i) * rows, rows)
                zb[part, :lanes], zb[part, lanes:] = split(out[:, i * lanes : (i + 1) * lanes])

    def trips(first, last):
        for n in range(first, last):
            for late_by, stage in ((3, spread_rows), (2, spread_lanes), (1, compare), (0, blur_rows)):
                if 0 <= n - late_by < len(groups):
                    stage(*groups[n - late_by])

    def inner_planes():
        trips(0, count)

    def outer_planes():
        trips(count, len(groups) + 3)

    def adjoint_z(ys):
        pair = [split(back_mid[pl.ds(y, sums, stride=pitch)]) for y in ys]
        high, low = (jnp.concatenate(part, 1) for part in zip(*pair))
        out = jnp.dot(za[:, :sums], high, preferred_element_type=f32)
        out = out[:planes] + out[planes:]
        out = out + jnp.dot(za[:planes, :sums], low, preferred_element_type=f32)
        for i, y in enumerate(ys):
            wide_out[pl.ds(y, planes, stride=pitch)] = out[:, i * lanes : (i + 1) * lanes]

    def pack_outer(step):
        def body(n, carry):
            for s in range(2):
                at = pitch * (n + (HALO + depth) * s)
                z_send[step, s, n, inner] = wide_out[pl.ds(at + HALO + 8, rows - 16)]
            return carry

        lax.fori_loop(0, HALO, body, 0)

    def pack_corners(step):
        def body(n, carry):
            for s in range(2):
                at = pitch * (n + (HALO + depth) * s)
                for r in range(2):
                    part = wide_out[pl.ds(at + (HALO + rows) * r, HALO)]
                    c_send[step, 2 * s + r, pl.ds(PAD + HALO * n, HALO)] = part
            return carry

        lax.fori_loop(0, HALO, body, 0)

    def pack_edges(phase):
        def body(n, carry):
            for s in range(2):
                for r in range(2):
                    at = pitch * (n + (HALO + depth) * s) + HALO + (rows - HALO) * r
                    part = wide_out[pl.ds(at, HALO)] + c_recv[phase, 2 * s + r, pl.ds(PAD + HALO * n, HALO)]
                    e_send[phase // 2, 2 * s + r, pl.ds(PAD + HALO * n, HALO)] = part
            return carry

        lax.fori_loop(0, HALO, body, 0)

    def pack_inner(phase):
        def body(p, carry):
            for r in range(2):
                strip = wide_out[pl.ds(pitch * (HALO + p) + (HALO + rows) * r, HALO)]
                y_send[phase, r, pl.ds(PAD + HALO * p, HALO)] = strip
            return carry

        lax.fori_loop(0, depth, body, 0)

    early = iota((16, lanes), 0) < HALO
    late = iota((16, lanes), 0) >= 16 - HALO

    def update(phase, target):
        def plane(p, s, n):
            value = wide_out[pl.ds(pitch * (HALO + p) + HALO, rows)]
            head, body, tail = value[:16], value[16 : rows - 16], value[rows - 16 :]
            first = y_recv[phase, 0, pl.ds(PAD + HALO * p, 16)]
            last = y_recv[phase, 1, pl.ds(1 + HALO * p, 16)]
            if s is not None:
                first = first + e_recv[phase, 2 * s, pl.ds(PAD + HALO * n, 16)]
                last = last + e_recv[phase, 2 * s + 1, pl.ds(1 + HALO * n, 16)]
                near = z_recv[phase, s, n]
                first = jnp.where(early, first, near[:16])
                last = jnp.where(late, last, near[rows - 16 :])
                body = body + near[16 : rows - 16]
            else:
                first = jnp.where(early, first, 0.0)
                last = jnp.where(late, last, 0.0)
            value = jnp.concatenate([head + first, body, tail + last], 0)
            target[p] = est[p] * value * (1.0 / count)

        def low(n, carry):
            plane(n, 0, n)
            return carry

        def central(n, carry):
            plane(n, None, None)
            return carry

        def high(n, carry):
            plane(top + n, 1, n)
            return carry

        lax.fori_loop(0, HALO, low, 0)
        lax.fori_loop(HALO, top, central, 0)
        lax.fori_loop(0, HALO, high, 0)

    for step in range(ITERS):
        ahead, back = 2 * step, 2 * step + 1
        gather_own()
        own_rows(lambda ys: forward_z(ys, inner_low, inner_high))
        if step > 0:
            receive(ahead, edges)
            send(ahead, corners)
        receive(ahead, faces_y)
        gather_y(ahead)
        rim_rows(lambda ys: forward_z(ys, inner_low, inner_high))
        inner_planes()
        receive(ahead, faces_z)
        gather_z(ahead)
        own_rows(lambda ys: forward_z(ys, outer_low, outer_high))
        receive(ahead, corners)
        gather_corners(ahead)
        rim_rows(lambda ys: forward_z(ys, outer_low, outer_high))
        outer_planes()
        rim_rows(adjoint_z)
        pack_corners(step)
        send(back, corners)
        pack_inner(back)
        send(back, faces_y)
        own_rows(adjoint_z)
        pack_outer(step)
        send(back, faces_z)
        receive(back, corners)
        pack_edges(back)
        send(back, edges)
        receive(back, faces_y + faces_z + edges)
        sent(ahead, names)
        if step < ITERS - 1:
            update(back, est)
            pack(ahead + 2)
            send(ahead + 2, edges + faces_y + faces_z)
        else:
            update(back, out_ref)
        sent(back, names)


def solution(mesh):
    tiles, strips_count = mesh.shape["tile"], mesh.shape["view"]

    def on_device(estimate, views, background, psf_taps, psf_lengths, view_offsets, field_rows):
        count, depth, rows, lanes = views.shape
        reach = depth + 2 * HALO
        side = HALO * depth
        phases = 2 * ITERS
        pitch = rows + 2 * HALO + 1
        planes = -(-reach // 16) * 16
        tall = -(-(rows + 2 * HALO) // 16) * 16
        sums = count * depth
        anywhere = pl.BlockSpec(memory_space=pl.ANY)
        scalar = pl.BlockSpec(memory_space=pltpu.SMEM)
        v = pltpu.VMEM
        return pl.pallas_call(
            functools.partial(kernel, tiles, strips_count),
            out_shape=jax.ShapeDtypeStruct((depth, rows, lanes), f32),
            in_specs=[anywhere, anywhere] + [scalar] * 5,
            out_specs=pl.BlockSpec(memory_space=pltpu.VMEM),
            scratch_shapes=[
                v((depth, rows, lanes), f32),
                v((count, depth, rows, lanes), f32),
                v((planes * pitch + 8, lanes), f32),
                v((-(-(sums * pitch + 16) // 64) * 64, lanes), f32),
                v((sums * pitch + 16, lanes), f32),
                v((planes * pitch + 8, lanes), f32),
                v((sums, 256), f32),
                v((planes, 256), f32),
                v((sums, 256), jnp.int32),
                v((planes, 256), jnp.int32),
                v((rows, 256), jnp.int32),
                v((rows, 256), jnp.int32),
                v((tall, 256), jnp.int32),
                v((tall, 256), jnp.int32),
                v((sums, 256), bf16),
                v((2 * planes, 256), bf16),
                v((count, rows, 256), bf16),
                v((count, tall, 256), bf16),
                v((count, 2 * lanes, 2 * lanes), bf16),
                v((count, 2 * lanes, 2 * lanes), bf16),
                v((2 * HALO * rows, 2 * lanes), bf16),
                v((2 * HALO * rows, 2 * lanes), bf16),
                v((2 * HALO * rows, lanes), bf16),
                v((2 * HALO * rows, lanes), bf16),
                v((ITERS, 2, HALO, rows, lanes), f32),
                v((phases, 2, side + 2 * PAD, lanes), f32),
                v((ITERS, 4, 104, lanes), f32),
                v((ITERS, 4, 104, lanes), f32),
                v((phases, 2, HALO, rows, lanes), f32),
                v((phases, 2, side + 2 * PAD, lanes), f32),
                v((phases, 4, 104, lanes), f32),
                v((phases, 4, 104, lanes), f32),
                pltpu.SemaphoreType.DMA((2,)),
                pltpu.SemaphoreType.DMA((phases, 12)),
                pltpu.SemaphoreType.DMA((phases, 12)),
            ],
            compiler_params=pltpu.CompilerParams(
                collective_id=0, has_side_effects=True, vmem_limit_bytes=60 * 2**20
            ),
            name="deconvolve",
        )(estimate, views, background, psf_taps, psf_lengths.T, view_offsets.T, field_rows.T)

    return jax.shard_map(
        on_device,
        mesh=mesh,
        in_specs=(P("tile", "view", None), P(None, "tile", "view", None), P(), P(), P(), P(), P()),
        out_specs=P("tile", "view", None),
        check_vma=False,
    )
```
